256 devices in a mesh: wide: 32 (over x, z_lo, y), narrow: 8 (over z_hi, core).
Axes of the slice: x: 4, y: 4, z: 8 (z_hi: 4, z_lo: 2; z = z_hi * 2 + z_lo), core: 2. Of those that a mesh axis runs over, the one named last changes fastest.
Arguments:
- inverse: bfloat16 [8192, 8192], P('wide', 'narrow')
- panel: bfloat16 [2, 8192, 4096], P(None, 'narrow', 'wide'), may hold values from -0.078125 to 0.078125
- factor_inv: bfloat16 [2, 4096, 4096], P(None, 'wide', 'narrow')
- structure: int32 [2, 24], replicated, may hold values from 0 to 31, as said below
Outputs:
- cross: bfloat16 [4096, 2, 8192], P('narrow', None, 'wide')
- variance: float32 [2, 4096], P(None, 'narrow')
The draws below stay inside these ranges and needn't reach their ends.
Inputs may be any that keep to these rules, and one draw needn't show every extreme that they name: `structure`: row k lists 24 distinct block indices in increasing order; the last, 31, is always listed.
All inputs are finite; a program needn't handle non-finite values.
Results may differ from the reference program's by a relative error of at most 0.0013.
Values may be sent and summed in bfloat16 or wider, within the bound.
A program may use at most 128 MiB of HBM per device.

```python
import math
import jax
import jax.numpy as jnp

KW = 4096
BLK = 256
NSUP = 2
NB = 32
NA = 8192
NSB = 24


def draw_inverse(key, part):
    key_off = jax.random.fold_in(key, 11)
    key_diag = jax.random.fold_in(key, 12)
    rough = jax.random.normal(key_off, (NA, NA), jnp.float32)
    lowest = 8.0
    highest = 64.0
    off_part = (rough + rough.T) * (12.0 / math.sqrt(2.0 * NA))
    diagonal = jnp.exp(jax.random.uniform(key_diag, (NA,), jnp.float32, math.log(lowest), math.log(highest)))
    identity = (jnp.arange(NA)[:, None] == jnp.arange(NA)[None, :]).astype(jnp.float32)
    return (off_part + identity * diagonal[None, :]).astype(jnp.bfloat16)


def draw_factor_inv(key, part):
    key_off = jax.random.fold_in(key, 21)
    key_diag = jax.random.fold_in(key, 22)
    rough = jax.random.normal(key_off, (NSUP, KW, KW), jnp.float32)
    lower = (jnp.arange(KW)[:, None] > jnp.arange(KW)[None, :]).astype(jnp.float32)
    identity = (jnp.arange(KW)[:, None] == jnp.arange(KW)[None, :]).astype(jnp.float32)
    diagonal = jnp.exp(jax.random.uniform(key_diag, (NSUP, 1, KW), jnp.float32, math.log(0.5), math.log(2.0)))
    values = rough * (2.0 / math.sqrt(KW)) * lower[None] + identity[None] * diagonal
    return values.astype(jnp.bfloat16)


def draw_structure(key, part):
    rows_list = []
    for sup_index in range(NSUP):
        shuffled = jax.random.permutation(jax.random.fold_in(key, 31 + sup_index), NB - 1)
        chosen = jnp.sort(shuffled[:NSB - 1].astype(jnp.int32))
        last_block = jnp.full((1,), NB - 1, jnp.int32)
        rows_list.append(jnp.concatenate([chosen, last_block]).astype(jnp.int32))
    return jnp.stack(rows_list)


def level_of(own_key, dims, split, low, largest):
    def one(position, blocks):
        heights = jax.random.uniform(jax.random.fold_in(jax.random.fold_in(own_key, 6), position), (blocks,), jnp.float32, low / len(split), largest / len(split))
        return jnp.repeat(jnp.exp(heights), dims[position] // blocks).reshape((-1,) + (1,) * (len(dims) - position - 1))

    factor_of = one(*split[0])
    for cut in split[1:]:
        factor_of = factor_of * one(*cut)
    return factor_of


def scatter_about(rng, extent, width, limit, pieces=(), held_as=jnp.bfloat16):
    result = jax.random.normal(rng, extent, jnp.float32) * width
    if len(pieces) > 0:
        result = level_of(rng, extent, pieces, -0.22, 0.18) * result
    return jnp.clip(result, min=-limit, max=limit).astype(held_as)


def setup_inputs(seed: int = 0) -> dict:
    keys = jax.random.split(jax.random.key(seed), 5)
    inverse = draw_inverse(jax.random.fold_in(keys[4], 71), 0)
    panel = scatter_about(keys[1], (NSUP, NA, KW), (NSB * BLK) ** -0.5, 0.078125, ((1, 8), (2, 32)))
    factor_inv = draw_factor_inv(jax.random.fold_in(keys[4], 71), 0)
    structure = draw_structure(jax.random.fold_in(keys[4], 71), 0)
    return dict(inverse=inverse, panel=panel, factor_inv=factor_inv, structure=structure)


def reference(inverse, panel, factor_inv, structure):
    block_ids = jnp.arange(NB, dtype=jnp.int32)
    in_structure = jnp.any(structure[:, :, None] == block_ids[None, None, :], axis=1)
    cross_list = []
    variance_list = []
    for sup_index in range(NSUP):
        row_mask = jnp.repeat(in_structure[sup_index], BLK).astype(jnp.float32)
        retained = (panel[sup_index].astype(jnp.float32) * row_mask[:, None]).astype(jnp.bfloat16)
        cross_part = -row_mask[:, None] * jnp.dot(inverse, retained, preferred_element_type=jnp.float32)
        linv_part = jnp.sum(jnp.square(factor_inv[sup_index].astype(jnp.float32)), axis=0)
        variance_list.append(linv_part - jnp.sum(panel[sup_index].astype(jnp.float32) * cross_part, axis=0))
        cross_list.append(cross_part.T.astype(jnp.bfloat16))
    return jnp.stack(cross_list, axis=1), jnp.stack(variance_list)
```

```python
import jax
import jax.numpy as jnp
from jax import lax
from jax.experimental import pallas as pl
from jax.experimental.pallas import tpu as pltpu
from jax.sharding import PartitionSpec as P

MESH = pl.DeviceIdType.MESH
BLK = 256
HALF = BLK // 2
NX, NZ, NY, NH, NC = 4, 2, 4, 4, 2


def kernel(
    negm_ref, s_ref, p_ref, l_ref, out_ref, var_ref,
    sg, pg, pv, acc, xacc, obuf, lsrc, lrecv, xsrc, xrecv, zsrc, zrecv, ysrc,
    ssem, rsem, lsem,
):
    w = lax.axis_index("wide")
    n = lax.axis_index("narrow")
    y = lax.rem(w, NY)
    zl = lax.rem(lax.div(w, NY), NZ)
    x = lax.div(w, NY * NZ)
    c = lax.rem(n, NC)
    h = lax.div(n, NC)

    def dev(x_=x, zl_=zl, y_=y, h_=h, c_=c):
        return ((x_ * NZ + zl_) * NY + y_, h_ * NC + c_)

    def xo(d):
        return lax.rem(x + d, NX)

    def yo(d):
        return lax.rem(y + d, NY)

    def ho(d):
        return lax.rem(h + d, NH)

    oz = 1 - zl
    oc = 1 - c
    swap = dev(x_=h, h_=x)
    stays = x == h
    moves = x != h

    barrier = pltpu.get_barrier_semaphore()
    partners = [dev(x_=xo(d)) for d in (1, 2, 3)] + [dev(y_=yo(d)) for d in (1, 2, 3)]
    partners += [dev(h_=ho(1)), dev(h_=ho(3)), dev(zl_=oz), dev(c_=oc)]
    for partner in partners:
        pl.semaphore_signal(barrier, inc=1, device_id=partner, device_id_type=MESH)

    @pl.when(moves)
    def _():
        pl.semaphore_signal(barrier, inc=1, device_id=swap, device_id_type=MESH)

    @pl.when(moves)
    def _():
        pl.semaphore_wait(barrier, len(partners) + 1)

    @pl.when(stays)
    def _():
        pl.semaphore_wait(barrier, len(partners))

    names = {}
    sent = []

    def remote(name, src, dst, device):
        i = names.setdefault(name, len(names))
        return pltpu.make_async_remote_copy(
            src_ref=src, dst_ref=dst, send_sem=ssem.at[i], recv_sem=rsem.at[i],
            device_id=device, device_id_type=MESH,
        )

    def send(name, src, dst, device):
        copy = remote(name, src, dst, device)
        copy.start()
        sent.append(copy)

    def arrived(name, landed):
        remote(name, landed, landed, dev(c_=oc)).wait_recv()

    top, bottom = pl.ds(0, HALF), pl.ds(HALF, HALF)
    half_of = {"t": top, "b": bottom}

    pt_local = pltpu.make_async_copy(p_ref, pg.at[x, zl], lsem.at[0])
    pt_remote = remote("pt", p_ref, pg.at[h, zl], swap)

    @pl.when(stays)
    def _():
        pt_local.start()

    @pl.when(moves)
    def _():
        pt_remote.start()

    s_local = pltpu.make_async_copy(s_ref, sg.at[h, y], lsem.at[1])
    s_local.start()

    def z_send(direction, half):
        name = ("z", direction, half)
        rows = half_of[half]
        target = dev(h_=ho(1 if direction == "+" else 3))
        send(name, s_ref.at[rows], sg.at[h, y, rows], target)

    def y_send(d, direction, half):
        rows = half_of[half]
        target = dev(y_=yo(1 if direction == "+" else 3))
        src = s_ref.at[rows] if d == 0 else sg.at[ho(d), y, rows]
        send(("y", d, direction, half), src, sg.at[ho(d), y, rows], target)

    def y_arrived(d, direction, half):
        source = yo(3 if direction == "+" else 1)
        arrived(("y", d, direction, half), sg.at[ho(d), source, half_of[half]])

    def y_forward(d, direction):
        half, source, to = ("t", yo(3), yo(1)) if direction == "+" else ("b", yo(1), yo(3))
        y_arrived(d, direction, half)
        piece = sg.at[ho(d), source, half_of[half]]
        send(("yf", d, direction), piece, piece, dev(y_=to))

    def y_forwarded(d, direction):
        half = "t" if direction == "+" else "b"
        arrived(("yf", d, direction), sg.at[ho(d), yo(2), half_of[half]])

    z_send("+", "t")
    z_send("-", "b")
    y_send(0, "+", "t")
    y_send(0, "-", "b")
    z_send("+", "b")
    z_send("-", "t")
    y_send(0, "+", "b")
    y_send(0, "-", "t")

    for yy in range(NY):
        columns = pl.ds(yy * 128, 128)
        for k in range(2):
            squares = l_ref[k, :, columns].astype(jnp.float32)
            lsrc[yy, pl.ds(k, 1), :] = jnp.sum(squares * squares, axis=0, keepdims=True)
        lsrc[yy, pl.ds(2, 6), :] = jnp.zeros((6, 128), jnp.float32)
    lrecv[y] = lsrc[y]
    for d in (1, 2, 3):
        send(("l", d), lsrc.at[yo(d)], lrecv.at[y], dev(y_=yo(d)))

    y_forward(0, "+")
    y_forward(0, "-")

    @pl.when(stays)
    def _():
        pt_local.wait()

    @pl.when(moves)
    def _():
        pt_remote.wait_send()
        remote("pt", pg.at[x, zl], pg.at[x, zl], swap).wait_recv()

    def x_send(piece, label):
        for direction, d in (("+", 1), ("-", 3)):
            send(("x", direction, label), pg.at[x, piece], pg.at[x, piece], dev(x_=xo(d)))

    send("zl", pg.at[x, zl], pg.at[x, zl], dev(zl_=oz))
    x_send(zl, "own")

    arrived(("z", "+", "t"), sg.at[ho(3), y, top])
    y_send(3, "+", "t")
    y_send(3, "-", "t")
    send("zf+", sg.at[ho(3), y, top], sg.at[ho(3), y, top], dev(h_=ho(1)))
    arrived(("z", "-", "b"), sg.at[ho(1), y, bottom])
    y_send(1, "-", "b")
    y_send(1, "+", "b")
    send("zf-", sg.at[ho(1), y, bottom], sg.at[ho(1), y, bottom], dev(h_=ho(3)))

    arrived("zl", pg.at[x, oz])
    x_send(oz, "other")

    pv_local = pltpu.make_async_copy(pg.at[x, c], pv, lsem.at[2])
    pv_remote = remote("pv", pg.at[x, oc], pv, dev(c_=oc))

    @pl.when(c == zl)
    def _():
        pv_local.start()
        pv_remote.start()

    arrived(("z", "+", "b"), sg.at[ho(3), y, bottom])
    y_send(3, "-", "b")
    y_send(3, "+", "b")
    arrived(("z", "-", "t"), sg.at[ho(1), y, top])
    y_send(1, "+", "t")
    y_send(1, "-", "t")

    y_forward(3, "+")
    y_forward(1, "-")

    arrived(("x", "+", "own"), pg.at[xo(3), zl])
    send("xf+", pg.at[xo(3), zl], pg.at[xo(3), zl], dev(x_=xo(1)))

    arrived("zf+", sg.at[ho(2), y, top])
    y_send(2, "+", "t")
    y_send(2, "-", "t")
    arrived("zf-", sg.at[ho(2), y, bottom])
    y_send(2, "-", "b")
    y_send(2, "+", "b")

    y_forward(3, "-")
    y_forward(1, "+")

    arrived(("x", "-", "other"), pg.at[xo(1), oz])
    send("xf-", pg.at[xo(1), oz], pg.at[xo(1), oz], dev(x_=xo(3)))

    @pl.when(c == zl)
    def _():
        pv_local.wait()
        pv_remote.wait_send()

    @pl.when(c != zl)
    def _():
        pv_remote.wait_recv()

    arrived(("x", "-", "own"), pg.at[xo(1), zl])
    arrived(("x", "+", "other"), pg.at[xo(3), oz])
    arrived("xf+", pg.at[xo(2), zl])
    arrived("xf-", pg.at[xo(2), oz])

    def multiply(d, e):
        slab, row = ho(d), yo(e)
        for cc in range(NC):
            product = jnp.dot(sg[slab, row], pg[slab, cc], preferred_element_type=jnp.float32)
            if d == 0:
                acc[cc, row] = product
            else:
                acc[cc, row] += product

    def multiply_slab(d):
        def step(e, carry):
            multiply(d, e)
            return carry

        lax.fori_loop(0, NY, step, 0)

    def rest_arrived(d):
        y_arrived(d, "+", "b")
        y_arrived(d, "-", "t")
        y_forwarded(d, "+")
        y_forwarded(d, "-")

    s_local.wait()
    rest_arrived(0)
    multiply_slab(0)
    y_forward(2, "+")
    y_forward(2, "-")
    rest_arrived(3)
    multiply_slab(3)
    rest_arrived(1)
    multiply_slab(1)

    def exchange(e):
        row = yo(e)
        send(("acc", e), acc.at[oc, row], xacc.at[row], dev(c_=oc))

    multiply(2, 0)
    exchange(0)
    y_arrived(2, "+", "b")
    multiply(2, 3)
    exchange(3)
    y_arrived(2, "-", "t")
    multiply(2, 1)
    exchange(1)
    y_forwarded(2, "+")
    y_forwarded(2, "-")
    multiply(2, 2)
    exchange(2)

    sums = [jnp.zeros((1, 128), jnp.float32) for _ in range(2)]
    own_columns = pl.ds(pl.multiple_of(y * 128, 128), 128)
    for e in (0, 3, 1, 2):
        row = yo(e)
        arrived(("acc", e), xacc.at[row])
        for k in range(2):
            lanes = pl.ds(k * 128, 128)
            total = acc[c, row, :, lanes] + xacc[row, :, lanes]
            value = total * negm_ref[k * NY + row]
            facing = pv[pl.ds(pl.multiple_of(row * BLK, BLK), BLK), lanes].astype(jnp.float32)
            sums[k] = sums[k] + jnp.sum(facing * value, axis=0, keepdims=True)
            turned = value.T.astype(jnp.bfloat16)
            if e == 0:
                out_ref[k, own_columns, :] = turned
            else:
                obuf[e, k] = turned
        if e != 0:
            send(("out", e), obuf.at[e], out_ref.at[:, own_columns, :], dev(y_=row))

    for d in (1, 2, 3):
        arrived(("l", d), lrecv.at[yo(NY - d)])
    factor = lrecv[0] + lrecv[1] + lrecv[2] + lrecv[3]
    weighted = jnp.concatenate(sums + [jnp.zeros((6, 128), jnp.float32)], axis=0)
    xsrc[...] = factor - weighted
    xrecv[x] = xsrc[...]
    for d in (1, 2, 3):
        send(("vx", d), xsrc, xrecv.at[x], dev(x_=xo(d)))
    for d in (1, 2, 3):
        arrived(("vx", d), xrecv.at[xo(NX - d)])
    zsrc[...] = xrecv[0] + xrecv[1] + xrecv[2] + xrecv[3]
    send("vz", zsrc, zrecv, dev(zl_=oz))
    arrived("vz", zrecv)
    ysrc[...] = zsrc[...] + zrecv[...]
    var_ref[y] = ysrc[...]
    for d in (1, 2, 3):
        send(("vy", d), ysrc, var_ref.at[y], dev(y_=yo(d)))
    for d in (1, 2, 3):
        arrived(("vy", d), var_ref.at[yo(NY - d)])
        source_columns = pl.ds(pl.multiple_of(yo(NY - d) * 128, 128), 128)
        arrived(("out", d), out_ref.at[:, source_columns, :])
    for copy in sent:
        copy.wait_send()


COPIES = 64


def per_device(inverse, panel, factor_inv, structure):
    w = lax.axis_index("wide")
    n = lax.axis_index("narrow")
    blocks = inverse.shape[1] // BLK
    col_ids = n * blocks + jnp.arange(blocks, dtype=jnp.int32)
    col_inside = jnp.any(structure[:, :, None] == col_ids[None, None, :], axis=1)
    row_ids = lax.div(w, NY) * NY + jnp.arange(NY, dtype=jnp.int32)
    row_inside = jnp.any(structure[:, :, None] == row_ids[None, None, :], axis=1)
    negm = -row_inside.astype(jnp.float32).reshape(-1)
    keep = jnp.repeat(col_inside, BLK, axis=1)
    kept = jnp.where(keep[:, :, None], panel, 0).astype(panel.dtype)
    kept = jnp.concatenate([kept[0], kept[1]], axis=1)

    vmem = pl.BlockSpec(memory_space=pltpu.VMEM)
    bf16, f32 = jnp.bfloat16, jnp.float32
    out, var = pl.pallas_call(
        kernel,
        out_shape=(
            jax.ShapeDtypeStruct((2, 512, BLK), bf16),
            jax.ShapeDtypeStruct((NY, 8, 128), f32),
        ),
        in_specs=[pl.BlockSpec(memory_space=pltpu.SMEM), vmem, vmem, vmem],
        out_specs=(vmem, vmem),
        scratch_shapes=[
            pltpu.VMEM((NH, NY, BLK, 1024), bf16),
            pltpu.VMEM((NX, NZ, 1024, 256), bf16),
            pltpu.VMEM((1024, 256), bf16),
            pltpu.VMEM((NC, NY, BLK, 256), f32),
            pltpu.VMEM((NY, BLK, 256), f32),
            pltpu.VMEM((NY, 2, 128, BLK), bf16),
            pltpu.VMEM((NY, 8, 128), f32),
            pltpu.VMEM((NY, 8, 128), f32),
            pltpu.VMEM((8, 128), f32),
            pltpu.VMEM((NX, 8, 128), f32),
            pltpu.VMEM((8, 128), f32),
            pltpu.VMEM((8, 128), f32),
            pltpu.VMEM((8, 128), f32),
            pltpu.SemaphoreType.DMA((COPIES,)),
            pltpu.SemaphoreType.DMA((COPIES,)),
            pltpu.SemaphoreType.DMA((3,)),
        ],
        compiler_params=pltpu.CompilerParams(
            collective_id=0, has_side_effects=True, vmem_limit_bytes=48 * 1024 * 1024
        ),
    )(negm, inverse, kept, factor_inv)
    cross = jnp.transpose(out, (1, 0, 2))
    variance = jnp.transpose(var[:, :2, :], (1, 0, 2)).reshape(2, -1)
    return cross, variance


def solution(mesh):
    in_specs = (P("wide", "narrow"), P(None, "narrow", "wide"), P(None, "wide", "narrow"), P())
    out_specs = (P("narrow", None, "wide"), P(None, "narrow"))
    return jax.shard_map(
        per_device, mesh=mesh, in_specs=in_specs, out_specs=out_specs, check_vma=False
    )
```

```python
import jax
import jax.numpy as jnp
from jax import lax
from jax.experimental import pallas as pl
from jax.experimental.pallas import tpu as pltpu
from jax.sharding import PartitionSpec as P

MESH = pl.DeviceIdType.MESH
BLK = 256
HALF = BLK // 2
NX, NZ, NY, NH, NC = 4, 2, 4, 4, 2


def kernel(
    negm_ref, s_ref, p_ref, l_ref, out_ref, var_ref,
    sg, pg, st, pv, acc, xacc, obuf, lsrc, lrecv, xsrc, xrecv, zsrc, zrecv, ysrc,
    ssem, rsem, lsem,
):
    w = lax.axis_index("wide")
    n = lax.axis_index("narrow")
    y = lax.rem(w, NY)
    zl = lax.rem(lax.div(w, NY), NZ)
    x = lax.div(w, NY * NZ)
    c = lax.rem(n, NC)
    h = lax.div(n, NC)

    def dev(x_=x, zl_=zl, y_=y, h_=h, c_=c):
        return ((x_ * NZ + zl_) * NY + y_, h_ * NC + c_)

    def xo(d):
        return lax.rem(x + d, NX)

    def yo(d):
        return lax.rem(y + d, NY)

    def ho(d):
        return lax.rem(h + d, NH)

    oz = 1 - zl
    oc = 1 - c

    barrier = pltpu.get_barrier_semaphore()
    partners = [dev(x_=xo(d)) for d in (1, 2, 3)] + [dev(y_=yo(d)) for d in (1, 2, 3)]
    partners += [dev(h_=ho(d)) for d in (1, 2, 3)] + [dev(zl_=oz), dev(c_=oc)]
    for partner in partners:
        pl.semaphore_signal(barrier, inc=1, device_id=partner, device_id_type=MESH)

    pl.semaphore_wait(barrier, len(partners))

    names = {}
    sent = []

    def remote(name, src, dst, device):
        i = names.setdefault(name, len(names))
        return pltpu.make_async_remote_copy(
            src_ref=src, dst_ref=dst, send_sem=ssem.at[i], recv_sem=rsem.at[i],
            device_id=device, device_id_type=MESH,
        )

    def send(name, src, dst, device):
        copy = remote(name, src, dst, device)
        copy.start()
        sent.append(copy)

    def arrived(name, landed):
        remote(name, landed, landed, dev(c_=oc)).wait_recv()

    top, bottom = pl.ds(0, HALF), pl.ds(HALF, HALF)
    half_of = {"t": top, "b": bottom}

    own_quarter = p_ref.at[pl.ds(pl.multiple_of(x * BLK, BLK), BLK)]
    q_local = pltpu.make_async_copy(own_quarter, st.at[x], lsem.at[0])
    q_stays = pltpu.make_async_copy(st.at[h], pg.at[x, zl, h], lsem.at[3])

    def quarters_x():
        q_local.start()
        for d in (1, 3, 2):
            src = p_ref.at[pl.ds(pl.multiple_of(xo(d) * BLK, BLK), BLK)]
            send(("qx", d), src, st.at[x], dev(x_=xo(d)))

    def quarters_h():
        q_local.wait()
        for d in (1, 3, 2):
            arrived(("qx", d), st.at[xo(NX - d)])
        q_stays.start()
        for d in (2, 1, 3):
            send(("qh", d), st.at[ho(d)], pg.at[x, zl, h], dev(h_=ho(d)))

    def quarters_finish():
        q_stays.wait()
        for d in (1, 3, 2):
            arrived(("qh", d), pg.at[x, zl, ho(NH - d)])

    s_local = pltpu.make_async_copy(s_ref, sg.at[h, y], lsem.at[1])
    s_local.start()

    def z_send(direction, half):
        name = ("z", direction, half)
        rows = half_of[half]
        target = dev(h_=ho(1 if direction == "+" else 3))
        send(name, s_ref.at[rows], sg.at[h, y, rows], target)

    def y_send(d, direction, half):
        rows = half_of[half]
        target = dev(y_=yo(1 if direction == "+" else 3))
        src = s_ref.at[rows] if d == 0 else sg.at[ho(d), y, rows]
        send(("y", d, direction, half), src, sg.at[ho(d), y, rows], target)

    def y_arrived(d, direction, half):
        source = yo(3 if direction == "+" else 1)
        arrived(("y", d, direction, half), sg.at[ho(d), source, half_of[half]])

    def y_forward(d, direction):
        half, source, to = ("t", yo(3), yo(1)) if direction == "+" else ("b", yo(1), yo(3))
        y_arrived(d, direction, half)
        piece = sg.at[ho(d), source, half_of[half]]
        send(("yf", d, direction), piece, piece, dev(y_=to))

    def y_forwarded(d, direction):
        half = "t" if direction == "+" else "b"
        arrived(("yf", d, direction), sg.at[ho(d), yo(2), half_of[half]])

    z_send("+", "t")
    z_send("-", "b")
    quarters_x()
    for direction, half in (("+", "t"), ("-", "b"), ("+", "b"), ("-", "t")):
        y_send(0, direction, half)

    def x_send(piece, label):
        for direction, d in (("+", 1), ("-", 3)):
            send(("x", direction, label), pg.at[x, piece], pg.at[x, piece], dev(x_=xo(d)))

    def z_onward(direction, half):
        d = 3 if direction == "+" else 1
        arrived(("z", direction, half), sg.at[ho(d), y, half_of[half]])
        for way in ("+", "-") if half == "t" else ("-", "+"):
            y_send(d, way, half)

    def h_forward(direction):
        d, half = (3, "t") if direction == "+" else (1, "b")
        piece = sg.at[ho(d), y, half_of[half]]
        send(("zf", direction), piece, piece, dev(h_=ho(NH - d)))

    def h_forwarded(direction):
        half = "t" if direction == "+" else "b"
        arrived(("zf", direction), sg.at[ho(2), y, half_of[half]])
        for way in ("+", "-") if half == "t" else ("-", "+"):
            y_send(2, way, half)

    quarters_h()
    z_onward("+", "t")
    z_onward("-", "b")

    for yy in range(NY):
        columns = pl.ds(yy * 128, 128)
        for k in range(2):
            squares = l_ref[k, :, columns].astype(jnp.float32)
            lsrc[yy, pl.ds(k, 1), :] = jnp.sum(squares * squares, axis=0, keepdims=True)
        lsrc[yy, pl.ds(2, 6), :] = jnp.zeros((6, 128), jnp.float32)
    lrecv[y] = lsrc[y]
    for d in (1, 2, 3):
        send(("l", d), lsrc.at[yo(d)], lrecv.at[y], dev(y_=yo(d)))

    y_forward(0, "+")
    y_forward(0, "-")
    z_send("+", "b")
    z_send("-", "t")

    quarters_finish()
    send("zl", pg.at[x, zl], pg.at[x, zl], dev(zl_=oz))
    x_send(zl, "own")

    z_onward("+", "b")
    z_onward("-", "t")
    h_forward("+")
    h_forward("-")

    y_forward(3, "+")
    y_forward(1, "-")

    arrived("zl", pg.at[x, oz])
    x_send(oz, "other")

    arrived(("x", "+", "own"), pg.at[xo(3), zl])
    send("xf+", pg.at[xo(3), zl], pg.at[xo(3), zl], dev(x_=xo(1)))

    h_forwarded("+")
    h_forwarded("-")

    y_forward(3, "-")
    y_forward(1, "+")

    arrived(("x", "-", "other"), pg.at[xo(1), oz])
    send("xf-", pg.at[xo(1), oz], pg.at[xo(1), oz], dev(x_=xo(3)))

    arrived(("x", "-", "own"), pg.at[xo(1), zl])
    arrived(("x", "+", "other"), pg.at[xo(3), oz])
    arrived("xf+", pg.at[xo(2), zl])
    arrived("xf-", pg.at[xo(2), oz])

    pv_local = pltpu.make_async_copy(pg.at[:, c, x], pv, lsem.at[2])
    pv_remote = remote("pv", pg.at[:, oc, x], pv, dev(c_=oc))

    @pl.when(c == zl)
    def _():
        pv_local.start()
        pv_remote.start()

    def multiply(d, e):
        slab, row = ho(d), yo(e)
        for cc in range(NC):
            product = jnp.dot(
                sg[slab, row, :, pl.ds(0, BLK)], pg[0, cc, slab], preferred_element_type=jnp.float32
            )
            for r in range(1, NX):
                product += jnp.dot(
                    sg[slab, row, :, pl.ds(r * BLK, BLK)], pg[r, cc, slab],
                    preferred_element_type=jnp.float32,
                )
            if d == 0:
                acc[cc, row] = product
            else:
                acc[cc, row] += product

    def multiply_slab(d):
        def step(e, carry):
            multiply(d, e)
            return carry

        lax.fori_loop(0, NY, step, 0)

    def rest_arrived(d):
        y_arrived(d, "+", "b")
        y_arrived(d, "-", "t")
        y_forwarded(d, "+")
        y_forwarded(d, "-")

    s_local.wait()
    rest_arrived(0)
    multiply_slab(0)
    y_forward(2, "+")
    y_forward(2, "-")
    rest_arrived(3)
    multiply_slab(3)
    rest_arrived(1)
    multiply_slab(1)

    def exchange(e):
        row = yo(e)
        send(("acc", e), acc.at[oc, row], xacc.at[row], dev(c_=oc))

    multiply(2, 0)
    exchange(0)
    y_arrived(2, "+", "b")
    multiply(2, 3)
    exchange(3)
    y_arrived(2, "-", "t")
    multiply(2, 1)
    exchange(1)
    y_forwarded(2, "+")
    y_forwarded(2, "-")
    multiply(2, 2)
    exchange(2)

    @pl.when(c == zl)
    def _():
        pv_local.wait()
        pv_remote.wait_send()

    @pl.when(c != zl)
    def _():
        pv_remote.wait_recv()

    sums = [jnp.zeros((1, 128), jnp.float32) for _ in range(2)]
    own_columns = pl.ds(pl.multiple_of(y * 128, 128), 128)
    for e in (0, 3, 1, 2):
        row = yo(e)
        arrived(("acc", e), xacc.at[row])
        for k in range(2):
            lanes = pl.ds(k * 128, 128)
            total = acc[c, row, :, lanes] + xacc[row, :, lanes]
            value = total * negm_ref[k * NY + row]
            facing = pv[row, :, lanes].astype(jnp.float32)
            sums[k] = sums[k] + jnp.sum(facing * value, axis=0, keepdims=True)
            turned = value.T.astype(jnp.bfloat16)
            if e == 0:
                out_ref[k, own_columns, :] = turned
            else:
                obuf[e, k] = turned
        if e != 0:
            send(("out", e), obuf.at[e], out_ref.at[:, own_columns, :], dev(y_=row))

    for d in (1, 2, 3):
        arrived(("l", d), lrecv.at[yo(NY - d)])
    factor = lrecv[0] + lrecv[1] + lrecv[2] + lrecv[3]
    weighted = jnp.concatenate(sums + [jnp.zeros((6, 128), jnp.float32)], axis=0)
    xsrc[...] = factor - weighted
    xrecv[x] = xsrc[...]
    for d in (1, 2, 3):
        send(("vx", d), xsrc, xrecv.at[x], dev(x_=xo(d)))
    for d in (1, 2, 3):
        arrived(("vx", d), xrecv.at[xo(NX - d)])
    zsrc[...] = xrecv[0] + xrecv[1] + xrecv[2] + xrecv[3]
    send("vz", zsrc, zrecv, dev(zl_=oz))
    arrived("vz", zrecv)
    ysrc[...] = zsrc[...] + zrecv[...]
    var_ref[y] = ysrc[...]
    for d in (1, 2, 3):
        send(("vy", d), ysrc, var_ref.at[y], dev(y_=yo(d)))
    for d in (1, 2, 3):
        arrived(("vy", d), var_ref.at[yo(NY - d)])
        source_columns = pl.ds(pl.multiple_of(yo(NY - d) * 128, 128), 128)
        arrived(("out", d), out_ref.at[:, source_columns, :])
    for copy in sent:
        copy.wait_send()


COPIES = 64


def per_device(inverse, panel, factor_inv, structure):
    w = lax.axis_index("wide")
    n = lax.axis_index("narrow")
    blocks = inverse.shape[1] // BLK
    col_ids = n * blocks + jnp.arange(blocks, dtype=jnp.int32)
    col_inside = jnp.any(structure[:, :, None] == col_ids[None, None, :], axis=1)
    row_ids = lax.div(w, NY) * NY + jnp.arange(NY, dtype=jnp.int32)
    row_inside = jnp.any(structure[:, :, None] == row_ids[None, None, :], axis=1)
    negm = -row_inside.astype(jnp.float32).reshape(-1)
    keep = jnp.repeat(col_inside, BLK, axis=1)
    kept = jnp.where(keep[:, :, None], panel, 0).astype(panel.dtype)
    kept = jnp.concatenate([kept[0], kept[1]], axis=1)

    vmem = pl.BlockSpec(memory_space=pltpu.VMEM)
    bf16, f32 = jnp.bfloat16, jnp.float32
    out, var = pl.pallas_call(
        kernel,
        out_shape=(
            jax.ShapeDtypeStruct((2, 512, BLK), bf16),
            jax.ShapeDtypeStruct((NY, 8, 128), f32),
        ),
        in_specs=[pl.BlockSpec(memory_space=pltpu.SMEM), vmem, vmem, vmem],
        out_specs=(vmem, vmem),
        scratch_shapes=[
            pltpu.VMEM((NH, NY, BLK, 1024), bf16),
            pltpu.VMEM((NX, NZ, NH, BLK, 256), bf16),
            pltpu.VMEM((NX, BLK, 256), bf16),
            pltpu.VMEM((NY, BLK, 256), bf16),
            pltpu.VMEM((NC, NY, BLK, 256), f32),
            pltpu.VMEM((NY, BLK, 256), f32),
            pltpu.VMEM((NY, 2, 128, BLK), bf16),
            pltpu.VMEM((NY, 8, 128), f32),
            pltpu.VMEM((NY, 8, 128), f32),
            pltpu.VMEM((8, 128), f32),
            pltpu.VMEM((NX, 8, 128), f32),
            pltpu.VMEM((8, 128), f32),
            pltpu.VMEM((8, 128), f32),
            pltpu.VMEM((8, 128), f32),
            pltpu.SemaphoreType.DMA((COPIES,)),
            pltpu.SemaphoreType.DMA((COPIES,)),
            pltpu.SemaphoreType.DMA((4,)),
        ],
        compiler_params=pltpu.CompilerParams(
            collective_id=0, has_side_effects=True, vmem_limit_bytes=48 * 1024 * 1024
        ),
    )(negm, inverse, kept, factor_inv)
    cross = jnp.transpose(out, (1, 0, 2))
    variance = jnp.transpose(var[:, :2, :], (1, 0, 2)).reshape(2, -1)
    return cross, variance


def solution(mesh):
    in_specs = (P("wide", "narrow"), P(None, "narrow", "wide"), P(None, "wide", "narrow"), P())
    out_specs = (P("narrow", None, "wide"), P(None, "narrow"))
    return jax.shard_map(
        per_device, mesh=mesh, in_specs=in_specs, out_specs=out_specs, check_vma=False
    )
```

```python
import jax
import jax.numpy as jnp
from jax import lax
from jax.experimental import pallas as pl
from jax.experimental.pallas import tpu as pltpu
from jax.sharding import PartitionSpec as P

MESH = pl.DeviceIdType.MESH
BLK = 256
HALF = BLK // 2
NX, NZ, NY, NH, NC = 4, 2, 4, 4, 2
NSUP = 2
NBLOCKS = 32
COPIES = 80
PLACE = {
    (0, 0): (0, 0), (0, 1): (1, 0), (3, 0): (0, 1), (3, 1): (0, 2),
    (1, 0): (1, 1), (1, 1): (1, 2), (2, 0): (1, 3), (2, 1): (0, 3),
}


def kernel(
    s_ref, p_ref, l_ref, struct_ref, out_ref, var_ref,
    sg, pg, st, pv, rhs, acc, xacc, obuf, lbuf, tbuf, mask, lsrc, lrecv, vsrc, vrecv, ysrc,
    ssem, rsem, lsem,
):
    w = lax.axis_index("wide")
    n = lax.axis_index("narrow")
    y = lax.rem(w, NY)
    zl = lax.rem(lax.div(w, NY), NZ)
    x = lax.div(w, NY * NZ)
    c = lax.rem(n, NC)
    h = lax.div(n, NC)
    oz = 1 - zl
    oc = 1 - c

    def dev(x_=x, zl_=zl, y_=y, h_=h, c_=c):
        return ((x_ * NZ + zl_) * NY + y_, h_ * NC + c_)

    def xo(d):
        return lax.rem(x + d, NX)

    def yo(d):
        return lax.rem(y + d, NY)

    def ho(d):
        return lax.rem(h + d, NH)

    s_local = pltpu.make_async_copy(s_ref, sg.at[h, y], lsem.at[1])
    l_local = pltpu.make_async_copy(l_ref, lbuf, lsem.at[4])
    t_local = pltpu.make_async_copy(struct_ref, tbuf, lsem.at[5])

    barrier = pltpu.get_barrier_semaphore()
    partners = [dev(x_=xo(d)) for d in (1, 2, 3)] + [dev(y_=yo(d)) for d in (1, 2, 3)]
    partners += [dev(h_=ho(1)), dev(h_=ho(3)), dev(zl_=oz), dev(c_=oc)]
    partners += [dev(h_=ho(3 - 2 * zl), zl_=oz), dev(h_=ho(2), zl_=oz)]
    partners += [dev(x_=xo(d), zl_=oz) for d in (1, 2, 3)]
    for partner in partners:
        pl.semaphore_signal(barrier, inc=1, device_id=partner, device_id_type=MESH)
    t_local.start()
    l_local.start()
    s_local.start()
    pl.semaphore_wait(barrier, len(partners))

    names = {("land", j): j for j in range(4)}
    sent = []

    def remote(name, src, dst, device):
        i = names.setdefault(name, len(names))
        return pltpu.make_async_remote_copy(
            src_ref=src, dst_ref=dst, send_sem=ssem.at[i], recv_sem=rsem.at[i],
            device_id=device, device_id_type=MESH,
        )

    def send(name, src, dst, device):
        copy = remote(name, src, dst, device)
        copy.start()
        sent.append(copy)

    def arrived(name, landed):
        remote(name, landed, landed, dev(c_=oc)).wait_recv()

    half_of = {"t": pl.ds(0, HALF), "b": pl.ds(HALF, HALF)}

    def quarter_of(r):
        return p_ref.at[:, pl.ds(pl.multiple_of(r * BLK, BLK), BLK), :]

    def place(d, cc):
        odd, two = lax.rem(d, 2), lax.div(d, 2)
        g = odd * (1 - two) + (1 - odd) * (cc + two * (1 - 2 * cc))
        return g, odd * (1 + cc) + (1 - odd) * two * 3

    q_local = pltpu.make_async_copy(quarter_of(x), st.at[x], lsem.at[0])
    q_stays = pltpu.make_async_copy(st.at[h], pg.at[x, zl, 0], lsem.at[3])

    def quarters_x():
        q_local.start()
        for d in (1, 3, 2):
            send(("qx", d), quarter_of(xo(d)), st.at[x], dev(x_=xo(d)))

    def quarter_send(d, g, j):
        i = names.setdefault(("qh", d), len(names))
        copy = pltpu.make_async_remote_copy(
            src_ref=st.at[ho(d)], dst_ref=pg.at[x, g, j], send_sem=ssem.at[i],
            recv_sem=rsem.at[j], device_id=dev(h_=ho(d), zl_=g), device_id_type=MESH,
        )
        copy.start()
        sent.append(copy)

    def quarters_h():
        q_local.wait()
        for d in (1, 3, 2):
            arrived(("qx", d), st.at[xo(NX - d)])
        q_stays.start()
        quarter_send(2, oz, 3)
        quarter_send(1, 0, 1 + zl)
        quarter_send(3, 1, 1 + zl)
        q_stays.wait()

    def quarters_finish():
        for j in (1, 2, 3):
            arrived(("land", j), pg.at[x, zl, j])

    def z_send(direction, half):
        rows = half_of[half]
        target = dev(h_=ho(1 if direction == "+" else 3))
        send(("z", direction, half), s_ref.at[rows], sg.at[h, y, rows], target)

    def y_send(d, direction, half):
        rows = half_of[half]
        target = dev(y_=yo(1 if direction == "+" else 3))
        src = s_ref.at[rows] if d == 0 else sg.at[ho(d), y, rows]
        send(("y", d, direction, half), src, sg.at[ho(d), y, rows], target)

    def y_arrived(d, direction, half):
        source = yo(3 if direction == "+" else 1)
        arrived(("y", d, direction, half), sg.at[ho(d), source, half_of[half]])

    def y_forward(d, direction):
        half, source, to = ("t", yo(3), yo(1)) if direction == "+" else ("b", yo(1), yo(3))
        y_arrived(d, direction, half)
        piece = sg.at[ho(d), source, half_of[half]]
        send(("yf", d, direction), piece, piece, dev(y_=to))

    def y_forwarded(d, direction):
        half = "t" if direction == "+" else "b"
        arrived(("yf", d, direction), sg.at[ho(d), yo(2), half_of[half]])

    def z_onward(direction, half):
        d = 3 if direction == "+" else 1
        arrived(("z", direction, half), sg.at[ho(d), y, half_of[half]])
        for way in ("+", "-") if half == "t" else ("-", "+"):
            y_send(d, way, half)

    def h_forward(direction):
        d, half = (3, "t") if direction == "+" else (1, "b")
        piece = sg.at[ho(d), y, half_of[half]]
        send(("zf", direction), piece, piece, dev(h_=ho(NH - d)))

    def h_forwarded(direction):
        half = "t" if direction == "+" else "b"
        arrived(("zf", direction), sg.at[ho(2), y, half_of[half]])
        for way in ("+", "-") if half == "t" else ("-", "+"):
            y_send(2, way, half)

    part_of = {"a": pl.ds(0, 1), "b": pl.ds(1, 3)}

    def zl_send(part):
        piece = pg.at[x, zl, part_of[part]]
        send(("zl", part), piece, piece, dev(zl_=oz))

    def zl_arrived(part):
        arrived(("zl", part), pg.at[x, oz, part_of[part]])

    def x_send(g, label, part):
        for direction, d in (("+", 1), ("-", 3)):
            piece = pg.at[x, g, part_of[part]]
            send(("x", direction, label, part), piece, piece, dev(x_=xo(d)))

    x_half = {"+": pl.ds(0, 2), "-": pl.ds(2, 2)}

    def x_forward(piece, label, direction):
        source = xo(3) if direction == "+" else xo(1)
        for part in ("a", "b"):
            arrived(("x", direction, label, part), pg.at[source, piece, part_of[part]])
        part = pg.at[source, piece, x_half[direction]]
        send(("xf", direction, label), part, part, dev(x_=xo(1 if direction == "+" else 3)))

    def x_forwarded(piece, label):
        for direction in ("+", "-"):
            arrived(("xf", direction, label), pg.at[xo(2), piece, x_half[direction]])

    z_send("+", "t")
    z_send("-", "b")
    quarters_x()
    for direction, half in (("+", "t"), ("-", "b"), ("+", "b"), ("-", "t")):
        y_send(0, direction, half)

    quarters_h()
    zl_send("a")
    x_send(zl, "own", "a")
    y_forward(0, "+")
    y_forward(0, "-")
    z_onward("+", "t")
    z_onward("-", "b")
    z_send("+", "b")
    z_send("-", "t")

    t_local.wait()
    ids = lax.broadcasted_iota(jnp.int32, (NBLOCKS, tbuf.shape[1]), 0)
    for k in range(NSUP):
        listed = jnp.where(ids == tbuf[pl.ds(k, 1), :], 1.0, 0.0)
        mask[k] = jnp.broadcast_to(jnp.max(listed, axis=1, keepdims=True), (NBLOCKS, 128))

    l_local.wait()
    for yy in range(NY):
        columns = pl.ds(yy * 128, 128)
        for k in range(NSUP):
            squares = lbuf[k, :, columns].astype(jnp.float32)
            lsrc[yy, pl.ds(k, 1), :] = jnp.sum(squares * squares, axis=0, keepdims=True)
        lsrc[yy, pl.ds(2, 6), :] = jnp.zeros((6, 128), jnp.float32)
    lrecv[y] = lsrc[y]
    for d in (1, 2, 3):
        send(("l", d), lsrc.at[yo(d)], lrecv.at[y], dev(y_=yo(d)))

    quarters_finish()
    zl_send("b")
    x_send(zl, "own", "b")
    zl_arrived("a")
    x_send(oz, "other", "a")

    y_forward(3, "+")
    y_forward(1, "-")

    z_onward("+", "b")
    z_onward("-", "t")

    x_forward(zl, "own", "+")
    x_forward(zl, "own", "-")
    h_forward("+")
    h_forward("-")

    zl_arrived("b")
    x_send(oz, "other", "b")

    y_forward(3, "-")
    y_forward(1, "+")

    h_forwarded("+")
    h_forwarded("-")

    x_forward(oz, "other", "+")
    x_forward(oz, "other", "-")
    x_forwarded(zl, "own")
    x_forwarded(oz, "other")

    apart = lax.rem(x - h + NH, NH)
    own_g, own_j = place(apart, c)
    other_g, other_j = place(apart, oc)
    pv_local = pltpu.make_async_copy(pg.at[:, own_g, own_j], pv, lsem.at[2])
    pv_remote = remote("pv", pg.at[:, other_g, other_j], pv, dev(c_=oc))

    @pl.when(c == zl)
    def _():
        pv_local.start()
        pv_remote.start()

    def prepare(d):
        slab = ho(d)
        for r in range(NX):
            block = (slab * NC + c) * NX + r
            for k in range(NSUP):
                keep = mask[k, pl.ds(block, 1), :].astype(jnp.bfloat16)
                for cc in range(NC):
                    g, j = PLACE[d, cc]
                    rhs[d, cc, pl.ds(r * BLK, BLK), pl.ds(k * 128, 128)] = pg[r, g, j, k] * keep

    def multiply(d, e):
        slab, row = ho(d), yo(e)
        for cc in range(NC):
            product = jnp.dot(sg[slab, row], rhs[d, cc], preferred_element_type=jnp.float32)
            if d == 0:
                acc[cc, row] = product
            else:
                acc[cc, row] += product

    def multiply_slab(d):
        def step(e, carry):
            multiply(d, e)
            return carry

        lax.fori_loop(0, NY, step, 0)

    def rest_arrived(d):
        y_arrived(d, "+", "b")
        y_arrived(d, "-", "t")
        y_forwarded(d, "+")
        y_forwarded(d, "-")

    s_local.wait()
    prepare(0)
    rest_arrived(0)
    multiply_slab(0)
    y_forward(2, "+")
    y_forward(2, "-")
    prepare(3)
    rest_arrived(3)
    multiply_slab(3)
    prepare(1)
    rest_arrived(1)
    multiply_slab(1)
    prepare(2)

    def exchange(e):
        row = yo(e)
        send(("acc", e), acc.at[oc, row], xacc.at[row], dev(c_=oc))

    multiply(2, 0)
    exchange(0)

    @pl.when(c == zl)
    def _():
        pv_local.wait()
        pv_remote.wait_send()

    @pl.when(c != zl)
    def _():
        pv_remote.wait_recv()

    sums = [jnp.zeros((1, 128), jnp.float32) for _ in range(NSUP)]
    own_columns = pl.ds(pl.multiple_of(y * 128, 128), 128)

    def finish(e):
        row = yo(e)
        arrived(("acc", e), xacc.at[row])
        block = (x * NZ + zl) * NY + row
        for k in range(NSUP):
            lanes = pl.ds(k * 128, 128)
            total = acc[c, row, :, lanes] + xacc[row, :, lanes]
            value = total * -mask[k, pl.ds(block, 1), :]
            facing = pv[row, k].astype(jnp.float32)
            sums[k] = sums[k] + jnp.sum(facing * value, axis=0, keepdims=True)
            turned = value.T.astype(jnp.bfloat16)
            if e == 0:
                out_ref[k, own_columns, :] = turned
            else:
                obuf[e, k] = turned
        if e != 0:
            send(("out", e), obuf.at[e], out_ref.at[:, own_columns, :], dev(y_=row))

    y_arrived(2, "+", "b")
    multiply(2, 3)
    exchange(3)
    y_arrived(2, "-", "t")
    multiply(2, 1)
    exchange(1)
    finish(0)
    finish(3)
    finish(1)
    for d in (1, 2, 3):
        arrived(("l", d), lrecv.at[yo(NY - d)])
    factor = lrecv[0] + lrecv[1] + lrecv[2] + lrecv[3]
    y_forwarded(2, "+")
    y_forwarded(2, "-")
    multiply(2, 2)
    exchange(2)
    finish(2)

    weighted = jnp.concatenate(sums + [jnp.zeros((6, 128), jnp.float32)], axis=0)
    vsrc[...] = factor - weighted
    others = [(d, z) for d in (2, 1, 3, 0) for z in (1, 0) if (d, z) != (0, 0)]
    for d, z in others:
        send(("v", d, z), vsrc, vrecv.at[x * NZ + zl], dev(x_=xo(d), zl_=oz if z else zl))
    vrecv[x * NZ + zl] = vsrc[...]
    for d, z in others:
        source = xo(NX - d) * NZ + (oz if z else zl)
        arrived(("v", d, z), vrecv.at[source])
    total = vrecv[0]
    for i in range(1, NX * NZ):
        total = total + vrecv[i]
    ysrc[...] = total
    var_ref[y] = total
    for d in (2, 1, 3):
        send(("vy", d), ysrc, var_ref.at[y], dev(y_=yo(d)))
    for d in (1, 3, 2):
        source_columns = pl.ds(pl.multiple_of(yo(NY - d) * 128, 128), 128)
        arrived(("out", d), out_ref.at[:, source_columns, :])
        arrived(("vy", d), var_ref.at[yo(NY - d)])
    for copy in sent:
        copy.wait_send()


def per_device(inverse, panel, factor_inv, structure):
    vmem = pl.BlockSpec(memory_space=pltpu.VMEM)
    hbm = pl.BlockSpec(memory_space=pltpu.HBM)
    bf16, f32 = jnp.bfloat16, jnp.float32
    out, var = pl.pallas_call(
        kernel,
        out_shape=(
            jax.ShapeDtypeStruct((NSUP, 512, BLK), bf16),
            jax.ShapeDtypeStruct((NY, 8, 128), f32),
        ),
        in_specs=[hbm, hbm, hbm, hbm],
        out_specs=(vmem, vmem),
        scratch_shapes=[
            pltpu.VMEM((NH, NY, BLK, 1024), bf16),
            pltpu.VMEM((NX, NZ, NH, NSUP, BLK, 128), bf16),
            pltpu.VMEM((NX, NSUP, BLK, 128), bf16),
            pltpu.VMEM((NY, NSUP, BLK, 128), bf16),
            pltpu.VMEM((NH, NC, 1024, 256), bf16),
            pltpu.VMEM((NC, NY, BLK, 256), f32),
            pltpu.VMEM((NY, BLK, 256), f32),
            pltpu.VMEM((NY, NSUP, 128, BLK), bf16),
            pltpu.VMEM(factor_inv.shape, bf16),
            pltpu.VMEM(structure.shape, jnp.int32),
            pltpu.VMEM((NSUP, NBLOCKS, 128), f32),
            pltpu.VMEM((NY, 8, 128), f32),
            pltpu.VMEM((NY, 8, 128), f32),
            pltpu.VMEM((8, 128), f32),
            pltpu.VMEM((NX * NZ, 8, 128), f32),
            pltpu.VMEM((8, 128), f32),
            pltpu.SemaphoreType.DMA((COPIES,)),
            pltpu.SemaphoreType.DMA((COPIES,)),
            pltpu.SemaphoreType.DMA((6,)),
        ],
        compiler_params=pltpu.CompilerParams(
            collective_id=0, has_side_effects=True, vmem_limit_bytes=60 * 1024 * 1024
        ),
    )(inverse, panel, factor_inv, structure)
    cross = jnp.transpose(out, (1, 0, 2))
    variance = jnp.transpose(var[:, :NSUP, :], (1, 0, 2)).reshape(NSUP, -1)
    return cross, variance


def solution(mesh):
    in_specs = (P("wide", "narrow"), P(None, "narrow", "wide"), P(None, "wide", "narrow"), P())
    out_specs = (P("narrow", None, "wide"), P(None, "narrow"))
    return jax.shard_map(
        per_device, mesh=mesh, in_specs=in_specs, out_specs=out_specs, check_vma=False
    )
```

```python
import jax
import jax.numpy as jnp
from jax import lax
from jax.experimental import pallas as pl
from jax.experimental.pallas import tpu as pltpu
from jax.sharding import PartitionSpec as P

MESH = pl.DeviceIdType.MESH
BLK = 256
HALF = BLK // 2
NX, NZ, NY, NH, NC = 4, 2, 4, 4, 2
NSUP = 2
NBLOCKS = 32
COPIES = 96
PLACE = {
    (0, 0): (0, 0), (0, 1): (1, 0), (3, 0): (0, 1), (3, 1): (0, 2),
    (1, 0): (1, 1), (1, 1): (1, 2), (2, 0): (1, 3), (2, 1): (0, 3),
}


def kernel(
    s_ref, p_ref, l_ref, struct_ref, out_ref, var_ref,
    sg, pg, st, pv, rhs, acc, xacc, obuf, lbuf, tbuf, mask, lsrc, lrecv, vsrc, vrecv, ysrc,
    ssem, rsem, lsem,
):
    w = lax.axis_index("wide")
    n = lax.axis_index("narrow")
    y = lax.rem(w, NY)
    zl = lax.rem(lax.div(w, NY), NZ)
    x = lax.div(w, NY * NZ)
    c = lax.rem(n, NC)
    h = lax.div(n, NC)
    oz = 1 - zl
    oc = 1 - c

    def dev(x_=x, zl_=zl, y_=y, h_=h, c_=c):
        return ((x_ * NZ + zl_) * NY + y_, h_ * NC + c_)

    def xo(d):
        return lax.rem(x + d, NX)

    def yo(d):
        return lax.rem(y + d, NY)

    def ho(d):
        return lax.rem(h + d, NH)

    s_local = pltpu.make_async_copy(s_ref, sg.at[h, y], lsem.at[1])
    l_local = pltpu.make_async_copy(l_ref, lbuf, lsem.at[4])
    t_local = pltpu.make_async_copy(struct_ref, tbuf, lsem.at[5])

    barrier = pltpu.get_barrier_semaphore()
    partners = [dev(x_=xo(d)) for d in (1, 2, 3)] + [dev(y_=yo(d)) for d in (1, 2, 3)]
    partners += [dev(h_=ho(1)), dev(h_=ho(3)), dev(zl_=oz), dev(c_=oc)]
    partners += [dev(h_=ho(3 - 2 * zl), zl_=oz), dev(h_=ho(2), zl_=oz)]
    partners += [dev(x_=xo(d), zl_=oz) for d in (1, 2, 3)]
    for partner in partners:
        pl.semaphore_signal(barrier, inc=1, device_id=partner, device_id_type=MESH)
    t_local.start()
    l_local.start()
    s_local.start()
    pl.semaphore_wait(barrier, len(partners))

    names = {("land", j): j for j in range(4)}
    sent = []

    def remote(name, src, dst, device):
        i = names.setdefault(name, len(names))
        return pltpu.make_async_remote_copy(
            src_ref=src, dst_ref=dst, send_sem=ssem.at[i], recv_sem=rsem.at[i],
            device_id=device, device_id_type=MESH,
        )

    def send(name, src, dst, device):
        copy = remote(name, src, dst, device)
        copy.start()
        sent.append(copy)

    def arrived(name, landed):
        remote(name, landed, landed, dev(c_=oc)).wait_recv()

    half_of = {"t": pl.ds(0, HALF), "b": pl.ds(HALF, HALF)}

    def quarter_of(r):
        return p_ref.at[:, pl.ds(pl.multiple_of(r * BLK, BLK), BLK), :]

    def place(d, cc):
        odd, two = lax.rem(d, 2), lax.div(d, 2)
        g = odd * (1 - two) + (1 - odd) * (cc + two * (1 - 2 * cc))
        return g, odd * (1 + cc) + (1 - odd) * two * 3

    q_local = pltpu.make_async_copy(quarter_of(x), st.at[x], lsem.at[0])
    q_stays = pltpu.make_async_copy(st.at[h], pg.at[x, zl, 0], lsem.at[3])

    def quarters_x():
        q_local.start()
        for d in (1, 3, 2):
            send(("qx", d), quarter_of(xo(d)), st.at[x], dev(x_=xo(d)))

    def quarter_send(d, g, j):
        i = names.setdefault(("qh", d), len(names))
        copy = pltpu.make_async_remote_copy(
            src_ref=st.at[ho(d)], dst_ref=pg.at[x, g, j], send_sem=ssem.at[i],
            recv_sem=rsem.at[j], device_id=dev(h_=ho(d), zl_=g), device_id_type=MESH,
        )
        copy.start()
        sent.append(copy)

    def quarters_h():
        q_local.wait()
        for d in (1, 3, 2):
            arrived(("qx", d), st.at[xo(NX - d)])
        q_stays.start()
        quarter_send(2, oz, 3)
        quarter_send(1, 0, 1 + zl)
        quarter_send(3, 1, 1 + zl)

    def z_send(direction, half):
        rows = half_of[half]
        target = dev(h_=ho(1 if direction == "+" else 3))
        send(("z", direction, half), s_ref.at[rows], sg.at[h, y, rows], target)

    def y_send(d, direction, half):
        rows = half_of[half]
        target = dev(y_=yo(1 if direction == "+" else 3))
        src = s_ref.at[rows] if d == 0 else sg.at[ho(d), y, rows]
        send(("y", d, direction, half), src, sg.at[ho(d), y, rows], target)

    def y_arrived(d, direction, half):
        source = yo(3 if direction == "+" else 1)
        arrived(("y", d, direction, half), sg.at[ho(d), source, half_of[half]])

    def y_forward(d, direction):
        half, source, to = ("t", yo(3), yo(1)) if direction == "+" else ("b", yo(1), yo(3))
        y_arrived(d, direction, half)
        piece = sg.at[ho(d), source, half_of[half]]
        send(("yf", d, direction), piece, piece, dev(y_=to))

    def y_forwarded(d, direction):
        half = "t" if direction == "+" else "b"
        arrived(("yf", d, direction), sg.at[ho(d), yo(2), half_of[half]])

    def z_onward(direction, half):
        d = 3 if direction == "+" else 1
        arrived(("z", direction, half), sg.at[ho(d), y, half_of[half]])
        for way in ("+", "-") if half == "t" else ("-", "+"):
            y_send(d, way, half)

    def h_forward(direction):
        d, half = (3, "t") if direction == "+" else (1, "b")
        piece = sg.at[ho(d), y, half_of[half]]
        send(("zf", direction), piece, piece, dev(h_=ho(NH - d)))

    def h_forwarded(direction):
        half = "t" if direction == "+" else "b"
        arrived(("zf", direction), sg.at[ho(2), y, half_of[half]])
        for way in ("+", "-") if half == "t" else ("-", "+"):
            y_send(2, way, half)

    def zl_send(j):
        send(("zl", j), pg.at[x, zl, j], pg.at[x, zl, j], dev(zl_=oz))

    def h_relay(direction):
        d, half = (3, "t") if direction == "+" else (1, "b")
        y_forwarded(d, direction)
        piece = sg.at[ho(d), yo(2), half_of[half]]
        send(("zg", direction), piece, piece, dev(h_=ho(NH - d)))

    def h_relayed(direction):
        half = "t" if direction == "+" else "b"
        arrived(("zg", direction), sg.at[ho(2), yo(2), half_of[half]])

    def x_send(g, label, j):
        for direction, d in (("+", 1), ("-", 3)):
            send(("x", direction, label, j), pg.at[x, g, j], pg.at[x, g, j], dev(x_=xo(d)))

    def own_panel(j):
        if j == 0:
            q_stays.wait()
        else:
            arrived(("land", j), pg.at[x, zl, j])
        zl_send(j)
        x_send(zl, "own", j)

    def other_panel(j):
        arrived(("zl", j), pg.at[x, oz, j])
        x_send(oz, "other", j)

    def x_forward(g, label, j):
        ahead, d = ("+", 1) if j in (0, 3) else ("-", 3)
        arrived(("x", ahead, label, j), pg.at[xo(NX - d), g, j])
        piece = pg.at[xo(NX - d), g, j]
        send(("xf", label, j), piece, piece, dev(x_=xo(d)))

    def x_near(g, label, j):
        behind, d = ("-", 3) if j in (0, 3) else ("+", 1)
        arrived(("x", behind, label, j), pg.at[xo(NX - d), g, j])

    def x_far(g, label, j):
        arrived(("xf", label, j), pg.at[xo(2), g, j])

    z_send("+", "t")
    z_send("-", "b")
    quarters_x()
    for direction, half in (("+", "t"), ("-", "b"), ("+", "b"), ("-", "t")):
        y_send(0, direction, half)

    quarters_h()
    own_panel(0)
    y_forward(0, "+")
    y_forward(0, "-")
    z_onward("+", "t")
    z_onward("-", "b")
    z_send("+", "b")
    z_send("-", "t")

    t_local.wait()
    ids = lax.broadcasted_iota(jnp.int32, (NBLOCKS, tbuf.shape[1]), 0)
    for k in range(NSUP):
        listed = jnp.where(ids == tbuf[pl.ds(k, 1), :], 1.0, 0.0)
        mask[k] = jnp.broadcast_to(jnp.max(listed, axis=1, keepdims=True), (NBLOCKS, 128))

    l_local.wait()
    for yy in range(NY):
        columns = pl.ds(yy * 128, 128)
        for k in range(NSUP):
            squares = lbuf[k, :, columns].astype(jnp.float32)
            lsrc[yy, pl.ds(k, 1), :] = jnp.sum(squares * squares, axis=0, keepdims=True)
        lsrc[yy, pl.ds(2, 6), :] = jnp.zeros((6, 128), jnp.float32)
    lrecv[y] = lsrc[y]
    for d in (1, 2, 3):
        send(("l", d), lsrc.at[yo(d)], lrecv.at[y], dev(y_=yo(d)))

    other_panel(0)
    x_forward(zl, "own", 0)
    own_panel(1)
    y_forward(3, "+")
    own_panel(3)
    y_forward(1, "-")
    own_panel(2)
    h_forward("+")
    h_forward("-")
    x_forward(oz, "other", 0)

    z_onward("+", "b")
    z_onward("-", "t")

    other_panel(1)
    x_forward(zl, "own", 1)
    y_forward(3, "-")
    other_panel(3)
    x_forward(zl, "own", 3)
    other_panel(2)
    x_forward(zl, "own", 2)
    y_forward(1, "+")
    x_forward(oz, "other", 1)

    h_forwarded("+")
    h_relay("+")
    x_forward(oz, "other", 3)
    h_forwarded("-")
    h_relay("-")
    x_forward(oz, "other", 2)
    NEAR, FAR = (0, 1, 3), (2,)

    def prepare(d, steps):
        for dr in steps:
            r = xo(dr)
            block = (ho(d) * NC + c) * NX + r
            for k in range(NSUP):
                keep = mask[k, pl.ds(block, 1), :].astype(jnp.bfloat16)
                for cc in range(NC):
                    g, j = PLACE[d, cc]
                    rhs[d, cc, dr, :, pl.ds(k * 128, 128)] = pg[r, g, j, k] * keep

    def multiply(d, e, steps, first=False):
        slab, row = ho(d), yo(e)
        for cc in range(NC):
            product = None
            for dr in steps:
                columns = pl.ds(pl.multiple_of(xo(dr) * BLK, BLK), BLK)
                term = jnp.dot(
                    sg[slab, row, :, columns], rhs[d, cc, dr], preferred_element_type=jnp.float32
                )
                product = term if product is None else product + term
            if first:
                acc[cc, row] = product
            else:
                acc[cc, row] += product

    def multiply_slab(d, steps, first=False):
        def step(e, carry):
            multiply(d, e, steps, first)
            return carry

        lax.fori_loop(0, NY, step, 0)

    def rest_arrived(d):
        y_arrived(d, "+", "b")
        y_arrived(d, "-", "t")

    for j in (0, 1, 3, 2):
        x_near(zl, "own", j)
        x_near(oz, "other", j)
    s_local.wait()
    prepare(0, NEAR)
    rest_arrived(0)
    y_forwarded(0, "+")
    y_forwarded(0, "-")
    multiply_slab(0, NEAR, first=True)
    prepare(3, NEAR)
    rest_arrived(3)
    y_forwarded(3, "-")
    multiply_slab(3, NEAR)
    prepare(1, NEAR)
    rest_arrived(1)
    y_forwarded(1, "+")
    multiply_slab(1, NEAR)
    prepare(2, NEAR)
    for j in (0, 1, 3, 2):
        x_far(zl, "own", j)
        x_far(oz, "other", j)

    apart = lax.rem(x - h + NH, NH)
    own_g, own_j = place(apart, c)
    other_g, other_j = place(apart, oc)
    pv_local = pltpu.make_async_copy(pg.at[:, own_g, own_j], pv, lsem.at[2])
    pv_remote = remote("pv", pg.at[:, other_g, other_j], pv, dev(c_=oc))

    @pl.when(c == zl)
    def _():
        pv_local.start()
        pv_remote.start()

    for d in (0, 3, 1):
        prepare(d, FAR)
        multiply_slab(d, FAR)
    prepare(2, FAR)
    ALL = (0, 1, 2, 3)

    def exchange(e):
        row = yo(e)
        send(("acc", e), acc.at[oc, row], xacc.at[row], dev(c_=oc))

    multiply(2, 0, ALL)
    exchange(0)

    @pl.when(c == zl)
    def _():
        pv_local.wait()
        pv_remote.wait_send()

    @pl.when(c != zl)
    def _():
        pv_remote.wait_recv()

    sums = [jnp.zeros((1, 128), jnp.float32) for _ in range(NSUP)]
    own_columns = pl.ds(pl.multiple_of(y * 128, 128), 128)

    def finish(e):
        row = yo(e)
        arrived(("acc", e), xacc.at[row])
        block = (x * NZ + zl) * NY + row
        for k in range(NSUP):
            lanes = pl.ds(k * 128, 128)
            total = acc[c, row, :, lanes] + xacc[row, :, lanes]
            value = total * -mask[k, pl.ds(block, 1), :]
            facing = pv[row, k].astype(jnp.float32)
            sums[k] = sums[k] + jnp.sum(facing * value, axis=0, keepdims=True)
            turned = value.T.astype(jnp.bfloat16)
            if e == 0:
                out_ref[k, own_columns, :] = turned
            else:
                obuf[e, k] = turned
        if e != 0:
            send(("out", e), obuf.at[e], out_ref.at[:, own_columns, :], dev(y_=row))

    y_arrived(2, "+", "t")
    y_arrived(2, "+", "b")
    multiply(2, 3, ALL)
    exchange(3)
    y_arrived(2, "-", "b")
    y_arrived(2, "-", "t")
    multiply(2, 1, ALL)
    exchange(1)
    finish(0)
    finish(3)
    finish(1)
    for d in (1, 2, 3):
        arrived(("l", d), lrecv.at[yo(NY - d)])
    factor = lrecv[0] + lrecv[1] + lrecv[2] + lrecv[3]
    h_relayed("+")
    h_relayed("-")
    multiply(2, 2, ALL)
    exchange(2)
    finish(2)

    weighted = jnp.concatenate(sums + [jnp.zeros((6, 128), jnp.float32)], axis=0)
    vsrc[...] = factor - weighted
    others = [(d, z) for d in (2, 1, 3, 0) for z in (1, 0) if (d, z) != (0, 0)]
    for d, z in others:
        send(("v", d, z), vsrc, vrecv.at[x * NZ + zl], dev(x_=xo(d), zl_=oz if z else zl))
    vrecv[x * NZ + zl] = vsrc[...]
    for d, z in others:
        source = xo(NX - d) * NZ + (oz if z else zl)
        arrived(("v", d, z), vrecv.at[source])
    total = vrecv[0]
    for i in range(1, NX * NZ):
        total = total + vrecv[i]
    ysrc[...] = total
    var_ref[y] = total
    for d in (2, 1, 3):
        send(("vy", d), ysrc, var_ref.at[y], dev(y_=yo(d)))
    for d in (1, 3, 2):
        source_columns = pl.ds(pl.multiple_of(yo(NY - d) * 128, 128), 128)
        arrived(("out", d), out_ref.at[:, source_columns, :])
        arrived(("vy", d), var_ref.at[yo(NY - d)])
    for copy in sent:
        copy.wait_send()


def per_device(inverse, panel, factor_inv, structure):
    vmem = pl.BlockSpec(memory_space=pltpu.VMEM)
    hbm = pl.BlockSpec(memory_space=pltpu.HBM)
    bf16, f32 = jnp.bfloat16, jnp.float32
    operands = [
        pltpu.with_memory_space_constraint(v, pltpu.HBM)
        for v in (inverse, panel, factor_inv, structure)
    ]
    out, var = pl.pallas_call(
        kernel,
        out_shape=(
            jax.ShapeDtypeStruct((NSUP, 512, BLK), bf16),
            jax.ShapeDtypeStruct((NY, 8, 128), f32),
        ),
        in_specs=[hbm, hbm, hbm, hbm],
        out_specs=(vmem, vmem),
        scratch_shapes=[
            pltpu.VMEM((NH, NY, BLK, 1024), bf16),
            pltpu.VMEM((NX, NZ, NH, NSUP, BLK, 128), bf16),
            pltpu.VMEM((NX, NSUP, BLK, 128), bf16),
            pltpu.VMEM((NY, NSUP, BLK, 128), bf16),
            pltpu.VMEM((NH, NC, NX, BLK, 256), bf16),
            pltpu.VMEM((NC, NY, BLK, 256), f32),
            pltpu.VMEM((NY, BLK, 256), f32),
            pltpu.VMEM((NY, NSUP, 128, BLK), bf16),
            pltpu.VMEM(factor_inv.shape, bf16),
            pltpu.VMEM(structure.shape, jnp.int32),
            pltpu.VMEM((NSUP, NBLOCKS, 128), f32),
            pltpu.VMEM((NY, 8, 128), f32),
            pltpu.VMEM((NY, 8, 128), f32),
            pltpu.VMEM((8, 128), f32),
            pltpu.VMEM((NX * NZ, 8, 128), f32),
            pltpu.VMEM((8, 128), f32),
            pltpu.SemaphoreType.DMA((COPIES,)),
            pltpu.SemaphoreType.DMA((COPIES,)),
            pltpu.SemaphoreType.DMA((6,)),
        ],
        compiler_params=pltpu.CompilerParams(
            collective_id=0, has_side_effects=True, vmem_limit_bytes=32 * 1024 * 1024
        ),
    )(*operands)
    cross = jnp.transpose(out, (1, 0, 2))
    variance = jnp.transpose(var[:, :NSUP, :], (1, 0, 2)).reshape(NSUP, -1)
    return cross, variance


def solution(mesh):
    in_specs = (P("wide", "narrow"), P(None, "narrow", "wide"), P(None, "wide", "narrow"), P())
    out_specs = (P("narrow", None, "wide"), P(None, "narrow"))
    return jax.shard_map(
        per_device, mesh=mesh, in_specs=in_specs, out_specs=out_specs, check_vma=False
    )
```

```python
import jax
import jax.numpy as jnp
from jax import lax
from jax.experimental import pallas as pl
from jax.experimental.pallas import tpu as pltpu
from jax.sharding import PartitionSpec as P

MESH = pl.DeviceIdType.MESH
BLK = 256
HALF = BLK // 2
NX, NZ, NY, NH, NC = 4, 2, 4, 4, 2
NSUP = 2
NBLOCKS = 32
COPIES = 96
TOWARD = 1


def kernel(
    s_ref, p_ref, l_ref, struct_ref, out_ref, var_ref,
    sg, pg, st, pv, rhs, acc, xacc, obuf, lbuf, tbuf, mask, lsrc, lrecv, vsrc, vrecv, ysrc,
    ssem, rsem, lsem,
):
    w = lax.axis_index("wide")
    n = lax.axis_index("narrow")
    y = lax.rem(w, NY)
    zl = lax.rem(lax.div(w, NY), NZ)
    x = lax.div(w, NY * NZ)
    c = lax.rem(n, NC)
    h = lax.div(n, NC)
    oz = 1 - zl
    oc = 1 - c

    def dev(x_=x, zl_=zl, y_=y, h_=h, c_=c):
        return ((x_ * NZ + zl_) * NY + y_, h_ * NC + c_)

    def xo(d):
        return lax.rem(x + d, NX)

    def yo(d):
        return lax.rem(y + d, NY)

    toward = TOWARD * (2 * zl - 1)

    def ho(d):
        return lax.rem(h + NH + toward * d, NH)

    s_local = pltpu.make_async_copy(s_ref, sg.at[h, y], lsem.at[1])
    l_local = pltpu.make_async_copy(l_ref, lbuf, lsem.at[4])
    t_local = pltpu.make_async_copy(struct_ref, tbuf, lsem.at[5])

    barrier = pltpu.get_barrier_semaphore()
    partners = [dev(x_=xo(d)) for d in (1, 2, 3)] + [dev(y_=yo(d)) for d in (1, 2, 3)]
    partners += [dev(h_=ho(1)), dev(h_=ho(3)), dev(zl_=oz), dev(c_=oc)]
    partners += [dev(h_=lax.rem(h + 3 + 2 * zl, NH), zl_=oz), dev(h_=ho(2), zl_=oz)]
    partners += [dev(x_=xo(d), zl_=oz) for d in (1, 2, 3)]
    for partner in partners:
        pl.semaphore_signal(barrier, inc=1, device_id=partner, device_id_type=MESH)
    t_local.start()
    l_local.start()
    s_local.start()
    pl.semaphore_wait(barrier, len(partners))

    names = {("land", j): j for j in range(4)}
    sent = []

    def remote(name, src, dst, device):
        i = names.setdefault(name, len(names))
        return pltpu.make_async_remote_copy(
            src_ref=src, dst_ref=dst, send_sem=ssem.at[i], recv_sem=rsem.at[i],
            device_id=device, device_id_type=MESH,
        )

    def send(name, src, dst, device):
        copy = remote(name, src, dst, device)
        copy.start()
        sent.append(copy)

    def arrived(name, landed):
        remote(name, landed, landed, dev(c_=oc)).wait_recv()

    half_of = {"t": pl.ds(0, HALF), "b": pl.ds(HALF, HALF)}

    def quarter_of(r):
        return p_ref.at[:, pl.ds(pl.multiple_of(r * BLK, BLK), BLK), :]

    def place(d, cc):
        odd, two = lax.rem(d, 2), lax.div(d, 2)
        g = odd * (1 - two) + (1 - odd) * (cc + two * (1 - 2 * cc))
        return g, odd * (1 + cc) + (1 - odd) * two * 3

    def nearer(d):
        return oz if (d == 1) == (TOWARD == 1) else zl

    def panel_place(d, cc):
        if d == 0:
            return cc, 0
        if d == 2:
            return 1 - cc, 3
        return (zl if (d == 1) == (TOWARD == 1) else oz), 1 + cc

    q_local = pltpu.make_async_copy(quarter_of(x), st.at[x], lsem.at[0])
    q_stays = pltpu.make_async_copy(st.at[h], pg.at[x, zl, 0], lsem.at[3])

    def quarters_x():
        q_local.start()
        for d in (1, 3, 2):
            send(("qx", d), quarter_of(xo(d)), st.at[x], dev(x_=xo(d)))

    def quarter_send(d, g, j):
        i = names.setdefault(("qh", d), len(names))
        copy = pltpu.make_async_remote_copy(
            src_ref=st.at[ho(d)], dst_ref=pg.at[x, g, j], send_sem=ssem.at[i],
            recv_sem=rsem.at[j], device_id=dev(h_=ho(d), zl_=g), device_id_type=MESH,
        )
        copy.start()
        sent.append(copy)

    def quarters_h():
        q_local.wait()
        for d in (1, 3, 2):
            arrived(("qx", d), st.at[xo(NX - d)])
        q_stays.start()
        quarter_send(2, oz, 3)
        quarter_send(1, nearer(1), 1 + zl)
        quarter_send(3, nearer(3), 1 + zl)

    def z_send(direction, half):
        rows = half_of[half]
        target = dev(h_=ho(1 if direction == "+" else 3))
        send(("z", direction, half), s_ref.at[rows], sg.at[h, y, rows], target)

    def y_send(d, direction, half):
        rows = half_of[half]
        target = dev(y_=yo(1 if direction == "+" else 3))
        src = s_ref.at[rows] if d == 0 else sg.at[ho(d), y, rows]
        send(("y", d, direction, half), src, sg.at[ho(d), y, rows], target)

    def y_arrived(d, direction, half):
        source = yo(3 if direction == "+" else 1)
        arrived(("y", d, direction, half), sg.at[ho(d), source, half_of[half]])

    def y_forward(d, direction):
        half, source, to = ("t", yo(3), yo(1)) if direction == "+" else ("b", yo(1), yo(3))
        y_arrived(d, direction, half)
        piece = sg.at[ho(d), source, half_of[half]]
        send(("yf", d, direction), piece, piece, dev(y_=to))

    def y_forwarded(d, direction):
        half = "t" if direction == "+" else "b"
        arrived(("yf", d, direction), sg.at[ho(d), yo(2), half_of[half]])

    def z_onward(direction, half):
        d = 3 if direction == "+" else 1
        arrived(("z", direction, half), sg.at[ho(d), y, half_of[half]])
        for way in ("+", "-") if half == "t" else ("-", "+"):
            y_send(d, way, half)

    def h_forward(direction):
        d, half = (3, "t") if direction == "+" else (1, "b")
        piece = sg.at[ho(d), y, half_of[half]]
        send(("zf", direction), piece, piece, dev(h_=ho(NH - d)))

    def h_forwarded(direction):
        half = "t" if direction == "+" else "b"
        arrived(("zf", direction), sg.at[ho(2), y, half_of[half]])
        for way in ("+", "-") if half == "t" else ("-", "+"):
            y_send(2, way, half)

    def h_relay(direction):
        d, half = (3, "t") if direction == "+" else (1, "b")
        y_forwarded(d, direction)
        piece = sg.at[ho(d), yo(2), half_of[half]]
        send(("zg", direction), piece, piece, dev(h_=ho(NH - d)))

    def h_relayed(direction):
        half = "t" if direction == "+" else "b"
        arrived(("zg", direction), sg.at[ho(2), yo(2), half_of[half]])

    index_of = {
        "own": {0: 0, "n": 1 + oz, "f": 1 + zl, 3: 3},
        "other": {0: 0, "n": 1 + zl, "f": 1 + oz, 3: 3},
    }
    group_of = {"own": zl, "other": oz}

    def panel_block(slot, label, j):
        return pg.at[slot, group_of[label], index_of[label][j]]

    def x_send(label, j):
        for direction, d in (("+", 1), ("-", 3)):
            piece = panel_block(x, label, j)
            send(("x", direction, label, j), piece, piece, dev(x_=xo(d)))

    def own_panel(j):
        piece = panel_block(x, "own", j)
        if j == 0:
            q_stays.wait()
        else:
            i = index_of["own"][j]
            pltpu.make_async_remote_copy(
                src_ref=piece, dst_ref=piece, send_sem=ssem.at[i], recv_sem=rsem.at[i],
                device_id=dev(c_=oc), device_id_type=MESH,
            ).wait_recv()
        send(("zl", j), piece, piece, dev(zl_=oz))
        x_send("own", j)

    def other_panel(j):
        arrived(("zl", j), panel_block(x, "other", j))
        x_send("other", j)

    AHEAD = (0, 3)

    def x_forward(label, j):
        ahead, d = ("+", 1) if j in AHEAD else ("-", 3)
        piece = panel_block(xo(NX - d), label, j)
        arrived(("x", ahead, label, j), piece)
        send(("xf", label, j), piece, piece, dev(x_=xo(d)))

    def x_near(label, j):
        behind, d = ("-", 3) if j in AHEAD else ("+", 1)
        arrived(("x", behind, label, j), panel_block(xo(NX - d), label, j))

    def x_far(label, j):
        arrived(("xf", label, j), panel_block(xo(2), label, j))

    NEAR, FAR, ALL = (0, 1, 3), (2,), (0, 1, 2, 3)

    def prepare(d, steps, cores=(0, 1)):
        for dr in steps:
            r = xo(dr)
            block = (ho(d) * NC + c) * NX + r
            for k in range(NSUP):
                keep = mask[k, pl.ds(block, 1), :].astype(jnp.bfloat16)
                for cc in cores:
                    g, j = panel_place(d, cc)
                    rhs[d, cc, dr, :, pl.ds(k * 128, 128)] = pg[r, g, j, k] * keep

    def multiply(d, e, steps, cores=(0, 1)):
        slab, row = ho(d), yo(e)
        for cc in cores:
            product = acc[cc, row]
            for dr in steps:
                columns = pl.ds(pl.multiple_of(xo(dr) * BLK, BLK), BLK)
                product += jnp.dot(
                    sg[slab, row, :, columns], rhs[d, cc, dr], preferred_element_type=jnp.float32
                )
            acc[cc, row] = product

    def multiply_slab(d, steps, cores=(0, 1), rows=NY):
        def step(e, carry):
            multiply(d, e, steps, cores)
            return carry

        lax.fori_loop(NY - rows, NY, step, 0)

    def rest_arrived(d):
        y_arrived(d, "+", "b")
        y_arrived(d, "-", "t")

    def early_products():
        for j in (0, "n", 3, "f"):
            x_near("own", j)
            x_far("own", j)
        prepare(0, ALL, (zl,))
        rest_arrived(0)
        y_forwarded(0, "+")
        y_forwarded(0, "-")
        multiply_slab(0, ALL, (zl,))
        prepare(1, ALL)
        rest_arrived(1)
        multiply(1, 0, ALL)
        multiply(1, 1, ALL)
        multiply(1, 3, ALL)

    z_send("+", "t")
    z_send("-", "b")
    quarters_x()
    y_send(0, "+", "t")
    y_send(0, "-", "b")
    y_send(0, "+", "b")
    y_send(0, "-", "t")
    quarters_h()
    own_panel(0)
    y_forward(0, "+")
    y_forward(0, "-")
    z_onward("+", "t")
    z_onward("-", "b")
    z_send("+", "b")
    z_send("-", "t")
    acc[...] = jnp.zeros_like(acc)
    s_local.wait()

    t_local.wait()
    ids = lax.broadcasted_iota(jnp.int32, (NBLOCKS, tbuf.shape[1]), 0)
    for k in range(NSUP):
        listed = jnp.where(ids == tbuf[pl.ds(k, 1), :], 1.0, 0.0)
        mask[k] = jnp.broadcast_to(jnp.max(listed, axis=1, keepdims=True), (NBLOCKS, 128))

    l_local.wait()
    for yy in range(NY):
        columns = pl.ds(yy * 128, 128)
        for k in range(NSUP):
            squares = lbuf[k, :, columns].astype(jnp.float32)
            lsrc[yy, pl.ds(k, 1), :] = jnp.sum(squares * squares, axis=0, keepdims=True)
    lrecv[y] = lsrc[y]
    for d in (1, 2, 3):
        send(("l", d), lsrc.at[yo(d)], lrecv.at[y], dev(y_=yo(d)))
    other_panel(0)
    x_forward("own", 0)
    y_forward(3, "+")
    y_forward(1, "-")
    own_panel("n")
    own_panel(3)
    own_panel("f")
    x_forward("other", 0)
    z_onward("+", "b")
    z_onward("-", "t")
    h_forward("+")
    h_forward("-")
    x_forward("own", "n")
    x_forward("own", 3)
    x_forward("own", "f")
    other_panel("n")
    y_forward(3, "-")
    other_panel(3)
    other_panel("f")
    y_forward(1, "+")
    x_forward("other", "n")
    h_forwarded("+")
    h_relay("+")
    x_forward("other", 3)
    early_products()
    h_forwarded("-")
    h_relay("-")
    x_forward("other", "f")

    for j in (0, "n", 3, "f"):
        x_near("other", j)
    prepare(0, NEAR, (oz,))
    multiply_slab(0, NEAR, (oz,))
    prepare(3, NEAR)
    rest_arrived(3)
    y_forwarded(3, "-")
    multiply_slab(3, NEAR)
    y_forwarded(1, "+")
    multiply(1, 2, ALL)
    prepare(2, NEAR)
    prepare(2, FAR, (oz,))
    for j in (0, "n", 3, "f"):
        x_far("other", j)

    apart = lax.rem(x - h + NH, NH)
    own_g, own_j = place(apart, c)
    other_g, other_j = place(apart, oc)
    pv_local = pltpu.make_async_copy(pg.at[:, own_g, own_j], pv, lsem.at[2])
    pv_remote = remote("pv", pg.at[:, other_g, other_j], pv, dev(c_=oc))

    @pl.when(c == zl)
    def _():
        pv_local.start()
        pv_remote.start()

    prepare(0, FAR, (oz,))
    multiply_slab(0, FAR, (oz,))
    prepare(3, FAR)
    multiply_slab(3, FAR)
    prepare(2, FAR, (zl,))

    def exchange(e):
        row = yo(e)
        send(("acc", e), acc.at[oc, row], xacc.at[row], dev(c_=oc))

    multiply(2, 0, ALL)
    exchange(0)

    @pl.when(c == zl)
    def _():
        pv_local.wait()
        pv_remote.wait_send()

    @pl.when(c != zl)
    def _():
        pv_remote.wait_recv()

    sums = [jnp.zeros((1, 128), jnp.float32) for _ in range(NSUP)]
    own_columns = pl.ds(pl.multiple_of(y * 128, 128), 128)

    def finish(e):
        row = yo(e)
        arrived(("acc", e), xacc.at[row])
        block = (x * NZ + zl) * NY + row
        for k in range(NSUP):
            lanes = pl.ds(k * 128, 128)
            total = acc[c, row, :, lanes] + xacc[row, :, lanes]
            value = total * -mask[k, pl.ds(block, 1), :]
            facing = pv[row, k].astype(jnp.float32)
            sums[k] = sums[k] + jnp.sum(facing * value, axis=0, keepdims=True)
            turned = value.T.astype(jnp.bfloat16)
            if e == 0:
                out_ref[k, own_columns, :] = turned
            else:
                obuf[e, k] = turned
        if e != 0:
            send(("out", e), obuf.at[e], out_ref.at[:, own_columns, :], dev(y_=row))

    y_arrived(2, "+", "t")
    y_arrived(2, "+", "b")
    multiply(2, 3, ALL)
    exchange(3)
    y_arrived(2, "-", "b")
    y_arrived(2, "-", "t")
    multiply(2, 1, ALL)
    exchange(1)
    for d in (1, 2, 3):
        arrived(("l", d), lrecv.at[yo(NY - d)])
    factor = lrecv[0] + lrecv[1] + lrecv[2] + lrecv[3]
    h_relayed("+")
    h_relayed("-")
    multiply(2, 2, ALL)
    exchange(2)
    finish(0)
    finish(3)
    finish(1)
    finish(2)

    weighted = jnp.concatenate(sums, axis=0)
    vsrc[...] = factor - weighted
    others = [(d, z) for d in (2, 1, 3, 0) for z in (1, 0) if (d, z) != (0, 0)]
    for d, z in others:
        send(("v", d, z), vsrc, vrecv.at[x * NZ + zl], dev(x_=xo(d), zl_=oz if z else zl))
    vrecv[x * NZ + zl] = vsrc[...]
    for d, z in others:
        source = xo(NX - d) * NZ + (oz if z else zl)
        arrived(("v", d, z), vrecv.at[source])
    total = vrecv[0]
    for i in range(1, NX * NZ):
        total = total + vrecv[i]
    ysrc[...] = total
    var_ref[:, own_columns] = total
    for d in (2, 1, 3):
        send(("vy", d), ysrc, var_ref.at[:, own_columns], dev(y_=yo(d)))
    for d in (1, 3, 2):
        source_columns = pl.ds(pl.multiple_of(yo(NY - d) * 128, 128), 128)
        arrived(("out", d), out_ref.at[:, source_columns, :])
        arrived(("vy", d), var_ref.at[:, source_columns])
    for copy in sent:
        copy.wait_send()


def per_device(inverse, panel, factor_inv, structure):
    vmem = pl.BlockSpec(memory_space=pltpu.VMEM)
    hbm = pl.BlockSpec(memory_space=pltpu.HBM)
    bf16, f32 = jnp.bfloat16, jnp.float32
    operands = [
        pltpu.with_memory_space_constraint(v, pltpu.HBM)
        for v in (inverse, panel, factor_inv, structure)
    ]
    out, var = pl.pallas_call(
        kernel,
        out_shape=(
            jax.ShapeDtypeStruct((NSUP, 512, BLK), bf16),
            jax.ShapeDtypeStruct((NSUP, 512), f32),
        ),
        in_specs=[hbm, hbm, hbm, hbm],
        out_specs=(vmem, vmem),
        scratch_shapes=[
            pltpu.VMEM((NH, NY, BLK, 1024), bf16),
            pltpu.VMEM((NX, NZ, NH, NSUP, BLK, 128), bf16),
            pltpu.VMEM((NX, NSUP, BLK, 128), bf16),
            pltpu.VMEM((NY, NSUP, BLK, 128), bf16),
            pltpu.VMEM((NH, NC, NX, BLK, 256), bf16),
            pltpu.VMEM((NC, NY, BLK, 256), f32),
            pltpu.VMEM((NY, BLK, 256), f32),
            pltpu.VMEM((NY, NSUP, 128, BLK), bf16),
            pltpu.VMEM(factor_inv.shape, bf16),
            pltpu.VMEM(structure.shape, jnp.int32),
            pltpu.VMEM((NSUP, NBLOCKS, 128), f32),
            pltpu.VMEM((NY, NSUP, 128), f32),
            pltpu.VMEM((NY, NSUP, 128), f32),
            pltpu.VMEM((NSUP, 128), f32),
            pltpu.VMEM((NX * NZ, NSUP, 128), f32),
            pltpu.VMEM((NSUP, 128), f32),
            pltpu.SemaphoreType.DMA((COPIES,)),
            pltpu.SemaphoreType.DMA((COPIES,)),
            pltpu.SemaphoreType.DMA((6,)),
        ],
        compiler_params=pltpu.CompilerParams(
            collective_id=0, has_side_effects=True, vmem_limit_bytes=32 * 1024 * 1024
        ),
    )(*operands)
    cross = jnp.transpose(out, (1, 0, 2))
    return cross, var


def solution(mesh):
    in_specs = (P("wide", "narrow"), P(None, "narrow", "wide"), P(None, "wide", "narrow"), P())
    out_specs = (P("narrow", None, "wide"), P(None, "narrow"))
    return jax.shard_map(
        per_device, mesh=mesh, in_specs=in_specs, out_specs=out_specs, check_vma=False
    )
```

```python
import jax
import jax.numpy as jnp
from jax import lax
from jax.experimental import pallas as pl
from jax.experimental.pallas import tpu as pltpu
from jax.sharding import PartitionSpec as P

MESH = pl.DeviceIdType.MESH
BLK = 256
HALF = BLK // 2
NX, NZ, NY, NH, NC = 4, 2, 4, 4, 2
NSUP = 2
NBLOCKS = 32
COPIES = 96
TOWARD = 1


def kernel(
    s_ref, p_ref, l_ref, struct_ref, out_ref, var_ref,
    sg, pg, st, pv, rhs, acc, xacc, obuf, lbuf, tbuf, mask, lsrc, lrecv, vsrc, vrecv, ysrc,
    ssem, rsem, lsem,
):
    w = lax.axis_index("wide")
    n = lax.axis_index("narrow")
    y = lax.rem(w, NY)
    zl = lax.rem(lax.div(w, NY), NZ)
    x = lax.div(w, NY * NZ)
    c = lax.rem(n, NC)
    h = lax.div(n, NC)
    oz = 1 - zl
    oc = 1 - c

    def dev(x_=x, zl_=zl, y_=y, h_=h, c_=c):
        return ((x_ * NZ + zl_) * NY + y_, h_ * NC + c_)

    def xo(d):
        return lax.rem(x + d, NX)

    def yo(d):
        return lax.rem(y + d, NY)

    toward = TOWARD * (2 * zl - 1)

    def ho(d):
        return lax.rem(h + NH + toward * d, NH)

    s_local = pltpu.make_async_copy(s_ref, sg.at[h, y], lsem.at[1])
    l_local = pltpu.make_async_copy(l_ref, lbuf, lsem.at[4])
    t_local = pltpu.make_async_copy(struct_ref, tbuf, lsem.at[5])

    barrier = pltpu.get_barrier_semaphore()
    partners = [dev(x_=xo(d)) for d in (1, 2, 3)] + [dev(y_=yo(d)) for d in (1, 2, 3)]
    partners += [dev(h_=ho(1)), dev(h_=ho(3)), dev(zl_=oz), dev(c_=oc)]
    partners += [dev(h_=lax.rem(h + 3 + 2 * zl, NH), zl_=oz), dev(h_=ho(2), zl_=oz)]
    partners += [dev(x_=xo(d), zl_=oz) for d in (1, 2, 3)]
    for partner in partners:
        pl.semaphore_signal(barrier, inc=1, device_id=partner, device_id_type=MESH)
    t_local.start()
    l_local.start()
    s_local.start()
    pl.semaphore_wait(barrier, len(partners))

    names = {("land", j): j for j in range(4)}
    sent = []

    def remote(name, src, dst, device):
        i = names.setdefault(name, len(names))
        return pltpu.make_async_remote_copy(
            src_ref=src, dst_ref=dst, send_sem=ssem.at[i], recv_sem=rsem.at[i],
            device_id=device, device_id_type=MESH,
        )

    def send(name, src, dst, device):
        copy = remote(name, src, dst, device)
        copy.start()
        sent.append(copy)

    def arrived(name, landed):
        remote(name, landed, landed, dev(c_=oc)).wait_recv()

    half_of = {"t": pl.ds(0, HALF), "b": pl.ds(HALF, HALF)}

    def quarter_of(r):
        return p_ref.at[:, pl.ds(pl.multiple_of(r * BLK, BLK), BLK), :]

    def place(d, cc):
        odd, two = lax.rem(d, 2), lax.div(d, 2)
        g = odd * (1 - two) + (1 - odd) * (cc + two * (1 - 2 * cc))
        return g, odd * (1 + cc) + (1 - odd) * two * 3

    def nearer(d):
        return oz if (d == 1) == (TOWARD == 1) else zl

    def panel_place(d, cc):
        if d == 0:
            return cc, 0
        if d == 2:
            return 1 - cc, 3
        return (zl if (d == 1) == (TOWARD == 1) else oz), 1 + cc

    q_local = pltpu.make_async_copy(quarter_of(x), st.at[x], lsem.at[0])
    q_stays = pltpu.make_async_copy(st.at[h], pg.at[x, zl, 0], lsem.at[3])

    def quarters_x():
        q_local.start()
        for d in (1, 3, 2):
            send(("qx", d), quarter_of(xo(d)), st.at[x], dev(x_=xo(d)))

    def quarter_send(d, g, j):
        i = names.setdefault(("qh", d), len(names))
        copy = pltpu.make_async_remote_copy(
            src_ref=st.at[ho(d)], dst_ref=pg.at[x, g, j], send_sem=ssem.at[i],
            recv_sem=rsem.at[j], device_id=dev(h_=ho(d), zl_=g), device_id_type=MESH,
        )
        copy.start()
        sent.append(copy)

    def quarters_h():
        q_local.wait()
        for d in (1, 3, 2):
            arrived(("qx", d), st.at[xo(NX - d)])
        q_stays.start()
        quarter_send(2, oz, 3)
        quarter_send(1, nearer(1), 1 + zl)
        quarter_send(3, nearer(3), 1 + zl)

    def z_send(direction, half):
        rows = half_of[half]
        target = dev(h_=ho(1 if direction == "+" else 3))
        send(("z", direction, half), s_ref.at[rows], sg.at[h, y, rows], target)

    def y_send(d, direction, half):
        rows = half_of[half]
        target = dev(y_=yo(1 if direction == "+" else 3))
        src = s_ref.at[rows] if d == 0 else sg.at[ho(d), y, rows]
        send(("y", d, direction, half), src, sg.at[ho(d), y, rows], target)

    def y_arrived(d, direction, half):
        source = yo(3 if direction == "+" else 1)
        arrived(("y", d, direction, half), sg.at[ho(d), source, half_of[half]])

    def y_forward(d, direction):
        half, source, to = ("t", yo(3), yo(1)) if direction == "+" else ("b", yo(1), yo(3))
        y_arrived(d, direction, half)
        piece = sg.at[ho(d), source, half_of[half]]
        send(("yf", d, direction), piece, piece, dev(y_=to))

    def y_forwarded(d, direction):
        half = "t" if direction == "+" else "b"
        arrived(("yf", d, direction), sg.at[ho(d), yo(2), half_of[half]])

    def z_onward(direction, half):
        d = 3 if direction == "+" else 1
        arrived(("z", direction, half), sg.at[ho(d), y, half_of[half]])
        for way in ("+", "-") if half == "t" else ("-", "+"):
            y_send(d, way, half)

    def h_forward(direction):
        d, half = (3, "t") if direction == "+" else (1, "b")
        piece = sg.at[ho(d), y, half_of[half]]
        send(("zf", direction), piece, piece, dev(h_=ho(NH - d)))

    def h_forwarded(direction):
        half = "t" if direction == "+" else "b"
        arrived(("zf", direction), sg.at[ho(2), y, half_of[half]])
        for way in ("+", "-") if half == "t" else ("-", "+"):
            y_send(2, way, half)

    def h_relay(direction):
        d, half = (3, "t") if direction == "+" else (1, "b")
        y_forwarded(d, direction)
        piece = sg.at[ho(d), yo(2), half_of[half]]
        send(("zg", direction), piece, piece, dev(h_=ho(NH - d)))

    def h_relayed(direction):
        half = "t" if direction == "+" else "b"
        arrived(("zg", direction), sg.at[ho(2), yo(2), half_of[half]])

    index_of = {
        "own": {0: 0, "n": 1 + oz, "f": 1 + zl, 3: 3},
        "other": {0: 0, "n": 1 + zl, "f": 1 + oz, 3: 3},
    }
    group_of = {"own": zl, "other": oz}

    def panel_block(slot, label, j):
        return pg.at[slot, group_of[label], index_of[label][j]]

    def x_send(label, j):
        for direction, d in (("+", 1), ("-", 3)):
            piece = panel_block(x, label, j)
            send(("x", direction, label, j), piece, piece, dev(x_=xo(d)))

    def own_panel(j):
        piece = panel_block(x, "own", j)
        if j == 0:
            q_stays.wait()
        else:
            i = index_of["own"][j]
            pltpu.make_async_remote_copy(
                src_ref=piece, dst_ref=piece, send_sem=ssem.at[i], recv_sem=rsem.at[i],
                device_id=dev(c_=oc), device_id_type=MESH,
            ).wait_recv()
        send(("zl", j), piece, piece, dev(zl_=oz))
        x_send("own", j)

    def other_panel(j):
        arrived(("zl", j), panel_block(x, "other", j))
        x_send("other", j)

    AHEAD = (0, 3)

    def x_forward(label, j):
        ahead, d = ("+", 1) if j in AHEAD else ("-", 3)
        piece = panel_block(xo(NX - d), label, j)
        arrived(("x", ahead, label, j), piece)
        send(("xf", label, j), piece, piece, dev(x_=xo(d)))

    def x_near(label, j):
        behind, d = ("-", 3) if j in AHEAD else ("+", 1)
        arrived(("x", behind, label, j), panel_block(xo(NX - d), label, j))

    def x_far(label, j):
        arrived(("xf", label, j), panel_block(xo(2), label, j))

    NEAR, FAR, ALL = (0, 1, 3), (2,), (0, 1, 2, 3)

    def prepare(d, steps, cores=(0, 1)):
        for dr in steps:
            r = xo(dr)
            block = (ho(d) * NC + c) * NX + r
            for k in range(NSUP):
                keep = mask[k, pl.ds(block, 1), :].astype(jnp.bfloat16)
                for cc in cores:
                    g, j = panel_place(d, cc)
                    rhs[d, cc, dr, :, pl.ds(k * 128, 128)] = pg[r, g, j, k] * keep

    def multiply(d, e, steps, cores=(0, 1)):
        slab, row = ho(d), yo(e)
        for cc in cores:
            product = acc[cc, row]
            for dr in steps:
                columns = pl.ds(pl.multiple_of(xo(dr) * BLK, BLK), BLK)
                product += jnp.dot(
                    sg[slab, row, :, columns], rhs[d, cc, dr], preferred_element_type=jnp.float32
                )
            acc[cc, row] = product

    def multiply_slab(d, steps, cores=(0, 1), rows=NY):
        def step(e, carry):
            multiply(d, e, steps, cores)
            return carry

        lax.fori_loop(NY - rows, NY, step, 0)

    def rest_arrived(d):
        y_arrived(d, "+", "b")
        y_arrived(d, "-", "t")

    def early_products():
        for j in (0, "n", 3, "f"):
            x_near("own", j)
            x_far("own", j)
        prepare(0, ALL, (zl,))
        rest_arrived(0)
        y_forwarded(0, "+")
        y_forwarded(0, "-")
        multiply_slab(0, ALL, (zl,))
        prepare(1, ALL)
        rest_arrived(1)
        multiply(1, 0, ALL)
        multiply(1, 1, ALL)
        multiply(1, 3, ALL)

    z_send("+", "t")
    z_send("-", "b")
    quarters_x()
    y_send(0, "+", "t")
    y_send(0, "-", "b")
    y_send(0, "+", "b")
    y_send(0, "-", "t")
    quarters_h()
    own_panel(0)
    y_forward(0, "+")
    y_forward(0, "-")
    z_onward("+", "t")
    z_onward("-", "b")
    z_send("+", "b")
    z_send("-", "t")
    acc[...] = jnp.zeros_like(acc)
    s_local.wait()

    t_local.wait()
    ids = lax.broadcasted_iota(jnp.int32, (NBLOCKS, tbuf.shape[1]), 0)
    for k in range(NSUP):
        listed = jnp.where(ids == tbuf[pl.ds(k, 1), :], 1.0, 0.0)
        mask[k] = jnp.broadcast_to(jnp.max(listed, axis=1, keepdims=True), (NBLOCKS, 128))

    l_local.wait()
    for yy in range(NY):
        columns = pl.ds(yy * 128, 128)
        for k in range(NSUP):
            squares = lbuf[k, :, columns].astype(jnp.float32)
            lsrc[yy, pl.ds(k, 1), :] = jnp.sum(squares * squares, axis=0, keepdims=True)
    lrecv[y] = lsrc[y]
    for d in (1, 2, 3):
        send(("l", d), lsrc.at[yo(d)], lrecv.at[y], dev(y_=yo(d)))
    other_panel(0)
    x_forward("own", 0)
    y_forward(3, "+")
    y_forward(1, "-")
    own_panel("n")
    own_panel(3)
    own_panel("f")
    x_forward("other", 0)
    z_onward("+", "b")
    z_onward("-", "t")
    h_forward("+")
    h_forward("-")
    x_forward("own", "n")
    x_forward("own", 3)
    x_forward("own", "f")
    other_panel("n")
    y_forward(3, "-")
    y_forward(1, "+")
    other_panel(3)
    other_panel("f")
    x_forward("other", "n")
    h_forwarded("+")
    h_relay("+")
    x_forward("other", 3)
    early_products()
    h_forwarded("-")
    h_relay("-")
    x_forward("other", "f")

    for j in (0, "n", 3, "f"):
        x_near("other", j)
    prepare(0, NEAR, (oz,))
    multiply_slab(0, NEAR, (oz,))
    prepare(3, NEAR)
    rest_arrived(3)
    y_forwarded(3, "-")
    multiply_slab(3, NEAR)
    y_forwarded(1, "+")
    multiply(1, 2, ALL)
    prepare(2, NEAR)
    prepare(2, FAR, (oz,))
    for j in (0, "n", 3, "f"):
        x_far("other", j)

    apart = lax.rem(x - h + NH, NH)
    own_g, own_j = place(apart, c)
    other_g, other_j = place(apart, oc)
    pv_local = pltpu.make_async_copy(pg.at[:, own_g, own_j], pv, lsem.at[2])
    pv_remote = remote("pv", pg.at[:, other_g, other_j], pv, dev(c_=oc))

    @pl.when(c == zl)
    def _():
        pv_local.start()
        pv_remote.start()

    prepare(0, FAR, (oz,))
    multiply_slab(0, FAR, (oz,))
    prepare(3, FAR)
    multiply_slab(3, FAR)
    prepare(2, FAR, (zl,))

    def exchange(e):
        row = yo(e)
        send(("acc", e), acc.at[oc, row], xacc.at[row], dev(c_=oc))

    multiply(2, 0, ALL)
    exchange(0)

    @pl.when(c == zl)
    def _():
        pv_local.wait()
        pv_remote.wait_send()

    @pl.when(c != zl)
    def _():
        pv_remote.wait_recv()

    sums = [jnp.zeros((1, 128), jnp.float32) for _ in range(NSUP)]
    own_columns = pl.ds(pl.multiple_of(y * 128, 128), 128)

    def finish(e):
        row = yo(e)
        arrived(("acc", e), xacc.at[row])
        block = (x * NZ + zl) * NY + row
        for k in range(NSUP):
            lanes = pl.ds(k * 128, 128)
            total = acc[c, row, :, lanes] + xacc[row, :, lanes]
            value = total * -mask[k, pl.ds(block, 1), :]
            facing = pv[row, k].astype(jnp.float32)
            sums[k] = sums[k] + jnp.sum(facing * value, axis=0, keepdims=True)
            turned = value.T.astype(jnp.bfloat16)
            if e == 0:
                out_ref[k, own_columns, :] = turned
            else:
                obuf[e, k] = turned
        if e != 0:
            send(("out", e), obuf.at[e], out_ref.at[:, own_columns, :], dev(y_=row))

    y_arrived(2, "+", "t")
    y_arrived(2, "+", "b")
    multiply(2, 3, ALL)
    exchange(3)
    finish(0)
    y_arrived(2, "-", "b")
    y_arrived(2, "-", "t")
    multiply(2, 1, ALL)
    exchange(1)
    finish(3)
    for d in (1, 2, 3):
        arrived(("l", d), lrecv.at[yo(NY - d)])
    factor = lrecv[0] + lrecv[1] + lrecv[2] + lrecv[3]
    h_relayed("+")
    h_relayed("-")
    multiply(2, 2, ALL)
    exchange(2)
    finish(1)
    finish(2)

    weighted = jnp.concatenate(sums, axis=0)
    vsrc[...] = factor - weighted
    others = [(d, z) for d in (2, 1, 3, 0) for z in (1, 0) if (d, z) != (0, 0)]
    for d, z in others:
        send(("v", d, z), vsrc, vrecv.at[x * NZ + zl], dev(x_=xo(d), zl_=oz if z else zl))
    vrecv[x * NZ + zl] = vsrc[...]
    for d, z in others:
        source = xo(NX - d) * NZ + (oz if z else zl)
        arrived(("v", d, z), vrecv.at[source])
    total = vrecv[0]
    for i in range(1, NX * NZ):
        total = total + vrecv[i]
    ysrc[...] = total
    var_ref[:, own_columns] = total
    for d in (2, 1, 3):
        send(("vy", d), ysrc, var_ref.at[:, own_columns], dev(y_=yo(d)))
    for d in (1, 3, 2):
        source_columns = pl.ds(pl.multiple_of(yo(NY - d) * 128, 128), 128)
        arrived(("out", d), out_ref.at[:, source_columns, :])
        arrived(("vy", d), var_ref.at[:, source_columns])
    for copy in sent:
        copy.wait_send()


def per_device(inverse, panel, factor_inv, structure):
    vmem = pl.BlockSpec(memory_space=pltpu.VMEM)
    hbm = pl.BlockSpec(memory_space=pltpu.HBM)
    bf16, f32 = jnp.bfloat16, jnp.float32
    operands = [
        pltpu.with_memory_space_constraint(v, pltpu.HBM)
        for v in (inverse, panel, factor_inv, structure)
    ]
    out, var = pl.pallas_call(
        kernel,
        out_shape=(
            jax.ShapeDtypeStruct((NSUP, 512, BLK), bf16),
            jax.ShapeDtypeStruct((NSUP, 512), f32),
        ),
        in_specs=[hbm, hbm, hbm, hbm],
        out_specs=(vmem, vmem),
        scratch_shapes=[
            pltpu.VMEM((NH, NY, BLK, 1024), bf16),
            pltpu.VMEM((NX, NZ, NH, NSUP, BLK, 128), bf16),
            pltpu.VMEM((NX, NSUP, BLK, 128), bf16),
            pltpu.VMEM((NY, NSUP, BLK, 128), bf16),
            pltpu.VMEM((NH, NC, NX, BLK, 256), bf16),
            pltpu.VMEM((NC, NY, BLK, 256), f32),
            pltpu.VMEM((NY, BLK, 256), f32),
            pltpu.VMEM((NY, NSUP, 128, BLK), bf16),
            pltpu.VMEM(factor_inv.shape, bf16),
            pltpu.VMEM(structure.shape, jnp.int32),
            pltpu.VMEM((NSUP, NBLOCKS, 128), f32),
            pltpu.VMEM((NY, NSUP, 128), f32),
            pltpu.VMEM((NY, NSUP, 128), f32),
            pltpu.VMEM((NSUP, 128), f32),
            pltpu.VMEM((NX * NZ, NSUP, 128), f32),
            pltpu.VMEM((NSUP, 128), f32),
            pltpu.SemaphoreType.DMA((COPIES,)),
            pltpu.SemaphoreType.DMA((COPIES,)),
            pltpu.SemaphoreType.DMA((6,)),
        ],
        compiler_params=pltpu.CompilerParams(
            collective_id=0, has_side_effects=True, vmem_limit_bytes=32 * 1024 * 1024
        ),
    )(*operands)
    cross = jnp.transpose(out, (1, 0, 2))
    return cross, var


def solution(mesh):
    in_specs = (P("wide", "narrow"), P(None, "narrow", "wide"), P(None, "wide", "narrow"), P())
    out_specs = (P("narrow", None, "wide"), P(None, "narrow"))
    return jax.shard_map(
        per_device, mesh=mesh, in_specs=in_specs, out_specs=out_specs, check_vma=False
    )
```

```python
import jax
import jax.numpy as jnp
from jax import lax
from jax.experimental import pallas as pl
from jax.experimental.pallas import tpu as pltpu
from jax.sharding import PartitionSpec as P

MESH = pl.DeviceIdType.MESH
BLK = 256
HALF = BLK // 2
NX, NZ, NY, NH, NC = 4, 2, 4, 4, 2
NSUP = 2
NBLOCKS = 32
COPIES = 96
TOWARD = 1


def kernel(
    s_ref, p_ref, l_ref, struct_ref, out_ref, var_ref,
    sg, pg, st, pv, rhs, acc, xacc, obuf, lbuf, tbuf, mask, lsrc, lrecv, vsrc, vrecv, ysrc,
    ssem, rsem, lsem,
):
    w = lax.axis_index("wide")
    n = lax.axis_index("narrow")
    y = lax.rem(w, NY)
    zl = lax.rem(lax.div(w, NY), NZ)
    x = lax.div(w, NY * NZ)
    c = lax.rem(n, NC)
    h = lax.div(n, NC)
    oz = 1 - zl
    oc = 1 - c

    def dev(x_=x, zl_=zl, y_=y, h_=h, c_=c):
        return ((x_ * NZ + zl_) * NY + y_, h_ * NC + c_)

    def xo(d):
        return lax.rem(x + d, NX)

    def yo(d):
        return lax.rem(y + d, NY)

    toward = TOWARD * (2 * zl - 1)

    def ho(d):
        return lax.rem(h + NH + toward * d, NH)

    s_local = pltpu.make_async_copy(s_ref, sg.at[h, y], lsem.at[1])
    l_local = pltpu.make_async_copy(l_ref, lbuf, lsem.at[4])
    t_local = pltpu.make_async_copy(struct_ref, tbuf, lsem.at[5])

    barrier = pltpu.get_barrier_semaphore()
    partners = [dev(x_=xo(d)) for d in (1, 2, 3)] + [dev(y_=yo(d)) for d in (1, 2, 3)]
    partners += [dev(h_=ho(1)), dev(h_=ho(3)), dev(zl_=oz), dev(c_=oc)]
    partners += [dev(h_=lax.rem(h + 3 + 2 * zl, NH), zl_=oz), dev(h_=ho(2), zl_=oz)]
    partners += [dev(x_=xo(d), zl_=oz) for d in (1, 2, 3)]
    for partner in partners:
        pl.semaphore_signal(barrier, inc=1, device_id=partner, device_id_type=MESH)
    t_local.start()
    l_local.start()
    s_local.start()
    pl.semaphore_wait(barrier, len(partners))

    names = {("land", j): j for j in range(4)}
    sent = []

    def remote(name, src, dst, device):
        i = names.setdefault(name, len(names))
        return pltpu.make_async_remote_copy(
            src_ref=src, dst_ref=dst, send_sem=ssem.at[i], recv_sem=rsem.at[i],
            device_id=device, device_id_type=MESH,
        )

    def send(name, src, dst, device):
        copy = remote(name, src, dst, device)
        copy.start()
        sent.append(copy)

    def arrived(name, landed):
        remote(name, landed, landed, dev(c_=oc)).wait_recv()

    half_of = {"t": pl.ds(0, HALF), "b": pl.ds(HALF, HALF)}

    def quarter_of(r):
        return p_ref.at[:, pl.ds(pl.multiple_of(r * BLK, BLK), BLK), :]

    def place(d, cc):
        odd, two = lax.rem(d, 2), lax.div(d, 2)
        g = odd * (1 - two) + (1 - odd) * (cc + two * (1 - 2 * cc))
        return g, odd * (1 + cc) + (1 - odd) * two * 3

    def nearer(d):
        return oz if (d == 1) == (TOWARD == 1) else zl

    def panel_place(d, cc):
        if d == 0:
            return cc, 0
        if d == 2:
            return 1 - cc, 3
        return (zl if (d == 1) == (TOWARD == 1) else oz), 1 + cc

    q_local = pltpu.make_async_copy(quarter_of(x), st.at[x], lsem.at[0])
    q_stays = pltpu.make_async_copy(st.at[h], pg.at[x, zl, 0], lsem.at[3])

    def quarters_x():
        q_local.start()
        for d in (1, 3, 2):
            send(("qx", d), quarter_of(xo(d)), st.at[x], dev(x_=xo(d)))

    def quarter_send(d, g, j):
        i = names.setdefault(("qh", d), len(names))
        copy = pltpu.make_async_remote_copy(
            src_ref=st.at[ho(d)], dst_ref=pg.at[x, g, j], send_sem=ssem.at[i],
            recv_sem=rsem.at[j], device_id=dev(h_=ho(d), zl_=g), device_id_type=MESH,
        )
        copy.start()
        sent.append(copy)

    def quarters_h():
        q_local.wait()
        for d in (1, 3, 2):
            arrived(("qx", d), st.at[xo(NX - d)])
        q_stays.start()
        quarter_send(2, oz, 3)
        quarter_send(1, nearer(1), 1 + zl)
        quarter_send(3, nearer(3), 1 + zl)

    def z_send(direction, half):
        rows = half_of[half]
        target = dev(h_=ho(1 if direction == "+" else 3))
        send(("z", direction, half), s_ref.at[rows], sg.at[h, y, rows], target)

    def y_send(d, direction, half):
        rows = half_of[half]
        target = dev(y_=yo(1 if direction == "+" else 3))
        src = s_ref.at[rows] if d == 0 else sg.at[ho(d), y, rows]
        send(("y", d, direction, half), src, sg.at[ho(d), y, rows], target)

    def y_arrived(d, direction, half):
        source = yo(3 if direction == "+" else 1)
        arrived(("y", d, direction, half), sg.at[ho(d), source, half_of[half]])

    def y_forward(d, direction):
        half, source, to = ("t", yo(3), yo(1)) if direction == "+" else ("b", yo(1), yo(3))
        y_arrived(d, direction, half)
        piece = sg.at[ho(d), source, half_of[half]]
        send(("yf", d, direction), piece, piece, dev(y_=to))

    def y_forwarded(d, direction):
        half = "t" if direction == "+" else "b"
        arrived(("yf", d, direction), sg.at[ho(d), yo(2), half_of[half]])

    def z_onward(direction, half):
        d = 3 if direction == "+" else 1
        arrived(("z", direction, half), sg.at[ho(d), y, half_of[half]])
        for way in ("+", "-") if half == "t" else ("-", "+"):
            y_send(d, way, half)

    def h_forward(direction):
        d, half = (3, "t") if direction == "+" else (1, "b")
        piece = sg.at[ho(d), y, half_of[half]]
        send(("zf", direction), piece, piece, dev(h_=ho(NH - d)))

    def h_forwarded(direction):
        half = "t" if direction == "+" else "b"
        arrived(("zf", direction), sg.at[ho(2), y, half_of[half]])
        for way in ("+", "-") if half == "t" else ("-", "+"):
            y_send(2, way, half)

    def h_relay(direction):
        d, half = (3, "t") if direction == "+" else (1, "b")
        y_forwarded(d, direction)
        piece = sg.at[ho(d), yo(2), half_of[half]]
        send(("zg", direction), piece, piece, dev(h_=ho(NH - d)))

    def h_relayed(direction):
        half = "t" if direction == "+" else "b"
        arrived(("zg", direction), sg.at[ho(2), yo(2), half_of[half]])

    index_of = {
        "own": {0: 0, "n": 1 + oz, "f": 1 + zl, 3: 3},
        "other": {0: 0, "n": 1 + zl, "f": 1 + oz, 3: 3},
    }
    group_of = {"own": zl, "other": oz}

    def panel_block(slot, label, j):
        return pg.at[slot, group_of[label], index_of[label][j]]

    def x_send(label, j):
        for direction, d in (("+", 1), ("-", 3)):
            piece = panel_block(x, label, j)
            send(("x", direction, label, j), piece, piece, dev(x_=xo(d)))

    def own_panel(j):
        piece = panel_block(x, "own", j)
        if j == 0:
            q_stays.wait()
        else:
            i = index_of["own"][j]
            pltpu.make_async_remote_copy(
                src_ref=piece, dst_ref=piece, send_sem=ssem.at[i], recv_sem=rsem.at[i],
                device_id=dev(c_=oc), device_id_type=MESH,
            ).wait_recv()
        send(("zl", j), piece, piece, dev(zl_=oz))
        x_send("own", j)

    def other_panel(j):
        arrived(("zl", j), panel_block(x, "other", j))
        x_send("other", j)

    AHEAD = (0, 3)

    def x_forward(label, j):
        ahead, d = ("+", 1) if j in AHEAD else ("-", 3)
        piece = panel_block(xo(NX - d), label, j)
        arrived(("x", ahead, label, j), piece)
        send(("xf", label, j), piece, piece, dev(x_=xo(d)))

    def x_near(label, j):
        behind, d = ("-", 3) if j in AHEAD else ("+", 1)
        arrived(("x", behind, label, j), panel_block(xo(NX - d), label, j))

    def x_far(label, j):
        arrived(("xf", label, j), panel_block(xo(2), label, j))

    NEAR, FAR, ALL = (0, 1, 3), (2,), (0, 1, 2, 3)

    def prepare(d, steps, cores=(0, 1)):
        for dr in steps:
            r = xo(dr)
            block = (ho(d) * NC + c) * NX + r
            for k in range(NSUP):
                keep = mask[k, pl.ds(block, 1), :].astype(jnp.bfloat16)
                for cc in cores:
                    g, j = panel_place(d, cc)
                    rhs[d, cc, dr, :, pl.ds(k * 128, 128)] = pg[r, g, j, k] * keep

    def multiply(d, e, steps, cores=(0, 1)):
        slab, row = ho(d), yo(e)
        for cc in cores:
            product = acc[cc, row]
            for dr in steps:
                columns = pl.ds(pl.multiple_of(xo(dr) * BLK, BLK), BLK)
                product += jnp.dot(
                    sg[slab, row, :, columns], rhs[d, cc, dr], preferred_element_type=jnp.float32
                )
            acc[cc, row] = product

    def multiply_slab(d, steps, cores=(0, 1), rows=NY):
        def step(e, carry):
            multiply(d, e, steps, cores)
            return carry

        lax.fori_loop(NY - rows, NY, step, 0)

    def rest_arrived(d):
        y_arrived(d, "+", "b")
        y_arrived(d, "-", "t")

    def early_products():
        for j in (0, "n", 3, "f"):
            x_near("own", j)
            x_far("own", j)
        prepare(0, ALL, (zl,))
        rest_arrived(0)
        y_forwarded(0, "+")
        y_forwarded(0, "-")
        multiply_slab(0, ALL, (zl,))
        prepare(1, ALL)
        rest_arrived(1)
        multiply(1, 0, ALL)
        multiply(1, 1, ALL)
        multiply(1, 3, ALL)

    z_send("+", "t")
    z_send("-", "b")
    quarters_x()
    y_send(0, "+", "t")
    y_send(0, "-", "b")
    y_send(0, "+", "b")
    y_send(0, "-", "t")
    quarters_h()
    own_panel(0)
    y_forward(0, "+")
    y_forward(0, "-")
    z_onward("+", "t")
    z_onward("-", "b")
    z_send("+", "b")
    z_send("-", "t")
    acc[...] = jnp.zeros_like(acc)
    s_local.wait()

    t_local.wait()
    ids = lax.broadcasted_iota(jnp.int32, (NBLOCKS, tbuf.shape[1]), 0)
    for k in range(NSUP):
        listed = jnp.where(ids == tbuf[pl.ds(k, 1), :], 1.0, 0.0)
        mask[k] = jnp.broadcast_to(jnp.max(listed, axis=1, keepdims=True), (NBLOCKS, 128))

    l_local.wait()
    for yy in range(NY):
        columns = pl.ds(yy * 128, 128)
        for k in range(NSUP):
            squares = lbuf[k, :, columns].astype(jnp.float32)
            lsrc[yy, pl.ds(k, 1), :] = jnp.sum(squares * squares, axis=0, keepdims=True)
    lrecv[y] = lsrc[y]
    for d in (1, 2, 3):
        send(("l", d), lsrc.at[yo(d)], lrecv.at[y], dev(y_=yo(d)))
    other_panel(0)
    x_forward("own", 0)
    y_forward(3, "+")
    y_forward(1, "-")
    own_panel("n")
    own_panel(3)
    own_panel("f")
    x_forward("other", 0)
    z_onward("+", "b")
    z_onward("-", "t")
    h_forward("+")
    h_forward("-")
    x_forward("own", "n")
    x_forward("own", 3)
    x_forward("own", "f")
    other_panel("n")
    y_forward(3, "-")
    y_forward(1, "+")
    other_panel(3)
    other_panel("f")
    x_forward("other", "n")
    h_forwarded("+")
    h_relay("+")
    x_forward("other", 3)
    early_products()
    h_forwarded("-")
    h_relay("-")
    x_forward("other", "f")

    for j in (0, "n", 3, "f"):
        x_near("other", j)
    prepare(0, NEAR, (oz,))
    multiply_slab(0, NEAR, (oz,))
    prepare(3, NEAR)
    rest_arrived(3)
    y_forwarded(3, "-")
    multiply_slab(3, NEAR)
    y_forwarded(1, "+")
    multiply(1, 2, ALL)
    prepare(2, NEAR)
    prepare(2, FAR, (oz,))
    for j in (0, "n", 3, "f"):
        x_far("other", j)

    apart = lax.rem(x - h + NH, NH)
    own_g, own_j = place(apart, c)
    other_g, other_j = place(apart, oc)
    pv_local = pltpu.make_async_copy(pg.at[:, own_g, own_j], pv, lsem.at[2])
    pv_remote = remote("pv", pg.at[:, other_g, other_j], pv, dev(c_=oc))

    @pl.when(c == zl)
    def _():
        pv_local.start()
        pv_remote.start()

    prepare(0, FAR, (oz,))
    multiply_slab(0, FAR, (oz,))
    prepare(3, FAR)
    multiply_slab(3, FAR)
    prepare(2, FAR, (zl,))

    def exchange(e):
        row = yo(e)
        send(("acc", e), acc.at[oc, row], xacc.at[row], dev(c_=oc))

    multiply(2, 0, ALL)
    exchange(0)

    @pl.when(c == zl)
    def _():
        pv_local.wait()
        pv_remote.wait_send()

    @pl.when(c != zl)
    def _():
        pv_remote.wait_recv()

    sums = [jnp.zeros((1, 128), jnp.float32) for _ in range(NSUP)]
    own_columns = pl.ds(pl.multiple_of(y * 128, 128), 128)

    def finish(e):
        row = yo(e)
        arrived(("acc", e), xacc.at[row])
        block = (x * NZ + zl) * NY + row
        turned = []
        for k in range(NSUP):
            lanes = pl.ds(k * 128, 128)
            total = acc[c, row, :, lanes] + xacc[row, :, lanes]
            value = total * -mask[k, pl.ds(block, 1), :]
            facing = pv[row, k].astype(jnp.float32)
            sums[k] = sums[k] + jnp.sum(facing * value, axis=0, keepdims=True)
            turned.append(value.T)
        both = jnp.stack(turned, axis=1).astype(jnp.bfloat16)
        if e == 0:
            out_ref[own_columns] = both
        else:
            obuf[e] = both
            send(("out", e), obuf.at[e], out_ref.at[own_columns], dev(y_=row))

    y_arrived(2, "+", "t")
    y_arrived(2, "+", "b")
    multiply(2, 3, ALL)
    exchange(3)
    finish(0)
    y_arrived(2, "-", "b")
    y_arrived(2, "-", "t")
    multiply(2, 1, ALL)
    exchange(1)
    finish(3)
    for d in (1, 2, 3):
        arrived(("l", d), lrecv.at[yo(NY - d)])
    factor = lrecv[0] + lrecv[1] + lrecv[2] + lrecv[3]
    h_relayed("+")
    h_relayed("-")
    multiply(2, 2, ALL)
    exchange(2)
    finish(1)
    finish(2)

    weighted = jnp.concatenate(sums, axis=0)
    vsrc[...] = factor - weighted
    others = [(d, z) for d in (2, 1, 3, 0) for z in (1, 0) if (d, z) != (0, 0)]
    for d, z in others:
        send(("v", d, z), vsrc, vrecv.at[x * NZ + zl], dev(x_=xo(d), zl_=oz if z else zl))
    vrecv[x * NZ + zl] = vsrc[...]
    for d, z in others:
        source = xo(NX - d) * NZ + (oz if z else zl)
        arrived(("v", d, z), vrecv.at[source])
    total = vrecv[0]
    for i in range(1, NX * NZ):
        total = total + vrecv[i]
    ysrc[...] = total
    var_ref[:, own_columns] = total
    for d in (2, 1, 3):
        send(("vy", d), ysrc, var_ref.at[:, own_columns], dev(y_=yo(d)))
    for d in (1, 3, 2):
        source_columns = pl.ds(pl.multiple_of(yo(NY - d) * 128, 128), 128)
        arrived(("out", d), out_ref.at[source_columns])
        arrived(("vy", d), var_ref.at[:, source_columns])
    for copy in sent:
        copy.wait_send()


def per_device(inverse, panel, factor_inv, structure):
    vmem = pl.BlockSpec(memory_space=pltpu.VMEM)
    hbm = pl.BlockSpec(memory_space=pltpu.HBM)
    bf16, f32 = jnp.bfloat16, jnp.float32
    operands = [
        pltpu.with_memory_space_constraint(v, pltpu.HBM)
        for v in (inverse, panel, factor_inv, structure)
    ]
    out, var = pl.pallas_call(
        kernel,
        out_shape=(
            jax.ShapeDtypeStruct((512, NSUP, BLK), bf16),
            jax.ShapeDtypeStruct((NSUP, 512), f32),
        ),
        in_specs=[hbm, hbm, hbm, hbm],
        out_specs=(vmem, vmem),
        scratch_shapes=[
            pltpu.VMEM((NH, NY, BLK, 1024), bf16),
            pltpu.VMEM((NX, NZ, NH, NSUP, BLK, 128), bf16),
            pltpu.VMEM((NX, NSUP, BLK, 128), bf16),
            pltpu.VMEM((NY, NSUP, BLK, 128), bf16),
            pltpu.VMEM((NH, NC, NX, BLK, 256), bf16),
            pltpu.VMEM((NC, NY, BLK, 256), f32),
            pltpu.VMEM((NY, BLK, 256), f32),
            pltpu.VMEM((NY, 128, NSUP, BLK), bf16),
            pltpu.VMEM(factor_inv.shape, bf16),
            pltpu.VMEM(structure.shape, jnp.int32),
            pltpu.VMEM((NSUP, NBLOCKS, 128), f32),
            pltpu.VMEM((NY, NSUP, 128), f32),
            pltpu.VMEM((NY, NSUP, 128), f32),
            pltpu.VMEM((NSUP, 128), f32),
            pltpu.VMEM((NX * NZ, NSUP, 128), f32),
            pltpu.VMEM((NSUP, 128), f32),
            pltpu.SemaphoreType.DMA((COPIES,)),
            pltpu.SemaphoreType.DMA((COPIES,)),
            pltpu.SemaphoreType.DMA((6,)),
        ],
        compiler_params=pltpu.CompilerParams(
            collective_id=0, has_side_effects=True, vmem_limit_bytes=32 * 1024 * 1024
        ),
    )(*operands)
    return out, var


def solution(mesh):
    in_specs = (P("wide", "narrow"), P(None, "narrow", "wide"), P(None, "wide", "narrow"), P())
    out_specs = (P("narrow", None, "wide"), P(None, "narrow"))
    return jax.shard_map(
        per_device, mesh=mesh, in_specs=in_specs, out_specs=out_specs, check_vma=False
    )
```
